512 devices in a mesh: dp: 16 (over x, z_lo), blk: 32 (over y, z_hi, core).
Axes of the slice: x: 4, y: 8, z: 8 (z_hi: 2, z_lo: 4; z = z_hi * 4 + z_lo), core: 2. Of those that a mesh axis runs over, the one named last changes fastest.
Arguments:
- query_rows: bfloat16 [16, 4096, 1024], P('dp', 'blk'), may hold values from -160 to 160
- key_rows: bfloat16 [16, 4096, 1024], P('dp', 'blk'), may hold values from -6 to 6
- value_rows: bfloat16 [16, 4096, 1024], P('dp', 'blk'), may hold values from -6 to 6
- grad_out: bfloat16 [16, 4096, 1024], P('dp', 'blk'), may hold values from -6 to 6
- pos_keys: bfloat16 [512, 1024], P('blk'), may hold values from -3 to 3
- bias_content: float32 [1024], replicated, may hold values from -3 to 3
- bias_position: float32 [1024], replicated, may hold values from -3 to 3
Outputs:
- query_gradient: bfloat16 [16, 4096, 1024], P('dp', 'blk')
- grad_key: bfloat16 [16, 4096, 1024], P('dp', 'blk')
- grad_value: bfloat16 [16, 4096, 1024], P('dp', 'blk')
- grad_pos_keys: float32 [512, 1024], P('blk')
The draws below stay inside these ranges and needn't reach their ends.
All inputs are finite; a program needn't handle non-finite values.
Results may differ from the reference program's by a relative error of at most 0.015.
The reference program's roundings to bfloat16 on the way (of `query_content`, `query_position`, `attention_b` and `dscore`) count: a program that leaves them out, or rounds other values in their place, can miss the bound.
Values may be sent and summed in bfloat16 or wider, within the bound.
A program may use at most 64 MiB of HBM per device.

```python
import jax
import jax.numpy as jnp
from jax import lax

H = 16
DH = 64
C = 128
D = 1024
BAND = 256
BATCH = 16
LEN = 4096
N_BLK = 32


def paired_fields(key):
    base_key = jax.random.fold_in(key, 11)
    key_query, key_keys = jax.random.split(base_key, 2)
    dims_all = (BATCH, LEN, D)
    query_field = jnp.clip(jax.random.normal(key_query, dims_all, jnp.float32), -5.0, 5.0)
    key_field = jnp.clip(jax.random.normal(key_keys, dims_all, jnp.float32), -5.0, 5.0)
    return (query_field, key_field)


def draw_query_rows(key, part):
    return paired_fields(key)[0].astype(jnp.bfloat16)


def draw_key_rows(key, part):
    return paired_fields(key)[1].astype(jnp.bfloat16)


def block_scale(rng, extent, cuts, low, top_value):
    loudness, own = 1.0, jax.random.fold_in(rng, 6)
    for dim, shards_of in cuts:
        draws = jnp.exp(jax.random.uniform(jax.random.fold_in(own, dim), (shards_of,), jnp.float32, low / len(cuts), top_value / len(cuts)))
        loudness = loudness * jnp.repeat(draws, extent[dim] // shards_of).reshape([-1 if axis == dim else 1 for axis in range(len(extent))])
    return loudness


def gaussian(stream_key, dims, scale, most, shards=(), kind=jnp.bfloat16):
    loudness = block_scale(stream_key, dims, shards, -0.22, 0.18) if shards else 1.0
    drawn = jax.random.normal(stream_key, dims, jnp.float32) * scale * loudness
    return jnp.minimum(jnp.maximum(drawn, -most), most).astype(kind)


def setup_inputs(seed: int = 0) -> dict:
    key_list = jax.random.split(jax.random.key(seed), 8)
    query_rows = draw_query_rows(jax.random.fold_in(key_list[7], 71), 0)
    key_rows = draw_key_rows(jax.random.fold_in(key_list[7], 71), 0)
    value_rows = gaussian(key_list[2], (BATCH, LEN, D), 1.0, 6.0, ((0, 16), (1, 32)))
    grad_out = gaussian(key_list[3], (BATCH, LEN, D), 1.0, 6.0, ((0, 16), (1, 32)))
    pos_keys = gaussian(key_list[4], (2 * BAND, D), 0.5, 3.0, ((0, 32),))
    bias_content = gaussian(key_list[5], (D,), 0.5, 3.0, (), jnp.float32)
    bias_position = gaussian(key_list[6], (D,), 0.5, 3.0, (), jnp.float32)
    return {"query_rows": query_rows, "key_rows": key_rows, "value_rows": value_rows, "grad_out": grad_out, "pos_keys": pos_keys, "bias_content": bias_content, "bias_position": bias_position}


def offset_table(frames):
    positions = jnp.arange(frames, dtype=jnp.int32)
    return (positions[:, None] - positions[None, :] + frames).astype(jnp.int32)


def relative_select(products):
    heads_count, frames = products.shape[0], products.shape[1]
    lookup = jnp.broadcast_to(offset_table(frames)[None], (heads_count, frames, frames))
    return jnp.take_along_axis(products, lookup, axis=2)


def relative_place(gradient, spread):
    heads_count, frames = gradient.shape[0], gradient.shape[1]
    positions = jnp.arange(frames, dtype=jnp.int32)
    zeroed = jnp.zeros((heads_count, frames, spread), gradient.dtype)
    return zeroed.at[:, positions[:, None], offset_table(frames)].set(gradient)


def split_heads(matrix):
    return matrix.reshape(matrix.shape[0], H, DH).astype(jnp.float32)


def join_head_axes(matrix):
    return matrix.reshape(matrix.shape[0], D)


def block_grads(query_content, query_position, own_keys, own_values, prev_keys, prev_values, grad_rows, band_own, band_prev):
    factor = DH ** -0.5
    content_h = split_heads(query_content)
    position_per_head = split_heads(query_position)
    keys_h = split_heads(jnp.concatenate([own_keys, prev_keys], axis=0))
    values_h = split_heads(jnp.concatenate([own_values, prev_values], axis=0))
    grad_h = split_heads(grad_rows)
    current_band_per_head = split_heads(band_own)
    earlier_band_per_head = split_heads(band_prev)
    content = jnp.einsum('ihd,jhd->hij', content_h, keys_h)
    current_position = relative_select(jnp.einsum('fju,tju->jft', position_per_head, current_band_per_head))
    earlier_position = relative_select(jnp.einsum('fju,tju->jft', position_per_head, earlier_band_per_head))
    scores = (content + jnp.concatenate([current_position, earlier_position], axis=2)) * factor
    row_max = jnp.max(scores, axis=2, keepdims=True)
    shifted = jnp.exp(scores - row_max)
    attention = shifted / jnp.sum(shifted, axis=2, keepdims=True)
    attention_b = lax.optimization_barrier(attention.astype(jnp.bfloat16))
    grad_weights = jnp.einsum('ihd,jhd->hij', grad_h, values_h)
    row_delta = jnp.sum(attention * grad_weights, axis=2, keepdims=True)
    dscore = lax.optimization_barrier((attention * (grad_weights - row_delta) * factor).astype(jnp.bfloat16))
    dscore_f = dscore.astype(jnp.float32)
    current_location = relative_place(dscore_f[:, :, :C], BAND)
    earlier_location = relative_place(dscore_f[:, :, C:], BAND)
    query_gradient = jnp.einsum('hij,jhd->ihd', dscore_f, keys_h)
    query_gradient = query_gradient + jnp.einsum('urk,kuo->ruo', current_location, current_band_per_head)
    query_gradient = query_gradient + jnp.einsum('urk,kuo->ruo', earlier_location, earlier_band_per_head)
    grad_keys = join_head_axes(jnp.einsum('hij,ihd->jhd', dscore_f, content_h))
    grad_values = join_head_axes(jnp.einsum('hij,ihd->jhd', attention_b.astype(jnp.float32), grad_h))
    current_band_gradient = join_head_axes(jnp.einsum('zfg,fzw->gzw', current_location, position_per_head))
    earlier_band_gradient = join_head_axes(jnp.einsum('zfg,fzw->gzw', earlier_location, position_per_head))
    return (join_head_axes(query_gradient).astype(jnp.bfloat16), grad_keys[:C], grad_keys[C:].astype(jnp.bfloat16),
            grad_values[:C], grad_values[C:].astype(jnp.bfloat16), current_band_gradient, earlier_band_gradient)


def reference(query_rows, key_rows, value_rows, grad_out, pos_keys, bias_content, bias_position):
    query_content = (query_rows.astype(jnp.float32) + bias_content).astype(jnp.bfloat16)
    query_position = (query_rows.astype(jnp.float32) + bias_position).astype(jnp.bfloat16)
    band_own = pos_keys[:BAND]
    band_prev = pos_keys[BAND:]

    def by_block(matrix):
        return matrix.reshape(BATCH * N_BLK, C, D)

    def previous(matrix):
        return jnp.roll(matrix.reshape(BATCH, N_BLK, C, D), 1, axis=1).reshape(BATCH * N_BLK, C, D)

    def to_owner(matrix):
        return jnp.roll(matrix.reshape(BATCH, N_BLK, C, D), -1, axis=1).reshape(BATCH, LEN, D)

    def step_one(band_sums, inputs):
        outcome = block_grads(*inputs, band_own, band_prev)
        return (band_sums[0] + outcome[5], band_sums[1] + outcome[6]), outcome[:5]

    initial = (jnp.zeros((BAND, D), jnp.float32), jnp.zeros((BAND, D), jnp.float32))
    band_sums, stacked = lax.scan(step_one, initial, (by_block(query_content), by_block(query_position),
                                                      by_block(key_rows), by_block(value_rows),
                                                      previous(key_rows), previous(value_rows), by_block(grad_out)))
    query_gradient = stacked[0].reshape(BATCH, LEN, D)
    key_part = lax.optimization_barrier(to_owner(stacked[2]))
    value_part = lax.optimization_barrier(to_owner(stacked[4]))
    grad_key = (stacked[1].reshape(BATCH, LEN, D) + key_part.astype(jnp.float32)).astype(jnp.bfloat16)
    grad_value = (stacked[3].reshape(BATCH, LEN, D) + value_part.astype(jnp.float32)).astype(jnp.bfloat16)
    grad_pos_keys = jnp.concatenate([band_sums[0], band_sums[1]], axis=0)
    return query_gradient, grad_key, grad_value, grad_pos_keys
```

```python
import functools

import jax
import jax.numpy as jnp
from jax import lax
from jax.experimental import pallas as pl
from jax.experimental.pallas import tpu as pltpu
from jax.sharding import PartitionSpec as P

MESH = pl.DeviceIdType.MESH
DH = 64
LANES = 2 * DH
FRAMES = 128
F32, BF16 = jnp.float32, jnp.bfloat16
NX, NY, NZ, ZL = 4, 8, 8, 4
QUERY, GRAD, KEY, VALUE = range(4)


def contract_lanes(a, b):
    return lax.dot_general(a, b, (((1,), (1,)), ((), ())), preferred_element_type=F32)


def contract_rows(a, b):
    return lax.dot_general(a, b, (((0,), (0,)), ((), ())), preferred_element_type=F32)


def place_roll(x):
    rows = x.shape[0]
    blocks = [
        pltpu.roll(x[8 * a : 8 * a + 8], (127 - 8 * a) % 128, 1) for a in range(rows // 8)
    ]
    x = jnp.concatenate(blocks, axis=0)
    row = lax.broadcasted_iota(jnp.int32, x.shape, 0)
    for bit in range(3):
        moved = pltpu.roll(x, 128 - 2**bit, 1)
        x = jnp.where(((row >> bit) & 1) == 1, moved, x)
    return x


def pair_grads(q, grad, keys, values, table, bias_c, bias_p):
    first = lax.broadcasted_iota(jnp.int32, (FRAMES, LANES), 1) < DH

    def stacked(x):
        zero = jnp.zeros_like(x)
        both = jnp.concatenate([jnp.where(first, x, zero), jnp.where(first, zero, x)], axis=0)
        return both.astype(BF16)

    q32 = q.astype(F32)
    content_in = stacked(q32 + bias_c)
    position_in = stacked(q32 + bias_p)
    grad_in = stacked(grad.astype(F32))
    content = contract_lanes(content_in, keys)
    spread = contract_lanes(position_in, table)
    weights = contract_lanes(grad_in, values)
    shape = (2 * FRAMES, FRAMES)
    frame = lax.broadcasted_iota(jnp.int32, shape, 0) & (FRAMES - 1)
    upper = lax.broadcasted_iota(jnp.int32, shape, 1) + frame >= FRAMES - 1

    def select(at):
        picked = jnp.where(upper, spread[:, at : at + 128], spread[:, at + 128 : at + 256])
        return pltpu.roll(picked, 1, 1, stride=1, stride_axis=0)

    factor = DH**-0.5
    s0 = (content[:, :128] + select(256)) * factor
    s1 = (content[:, 128:] + select(0)) * factor
    top = jnp.max(jnp.maximum(s0, s1), axis=1, keepdims=True)
    e0, e1 = jnp.exp(s0 - top), jnp.exp(s1 - top)
    inverse = 1.0 / jnp.sum(e0 + e1, axis=1, keepdims=True)
    a0, a1 = e0 * inverse, e1 * inverse
    w0, w1 = weights[:, :128], weights[:, 128:]
    delta = jnp.sum(a0 * w0 + a1 * w1, axis=1, keepdims=True)
    d0 = a0 * (w0 - delta) * factor
    d1 = a1 * (w1 - delta) * factor
    dscore = jnp.concatenate([d0, d1], axis=1).astype(BF16)
    attention = jnp.concatenate([a0, a1], axis=1).astype(BF16)
    p0, p1 = place_roll(d0), place_roll(d1)
    zero = jnp.zeros_like(p0)
    location = jnp.concatenate(
        [
            jnp.where(upper, p1, zero),
            jnp.where(upper, zero, p1),
            jnp.where(upper, p0, zero),
            jnp.where(upper, zero, p0),
        ],
        axis=1,
    ).astype(BF16)
    both = jnp.dot(
        jnp.concatenate([dscore, location], axis=1),
        jnp.concatenate([keys, table], axis=0),
        preferred_element_type=F32,
    )
    query_gradient = jnp.where(first, both[:FRAMES], both[FRAMES:])
    key_term = contract_rows(dscore, content_in)
    value_term = contract_rows(attention, grad_in)
    band_term = contract_rows(location, position_in)
    return query_gradient, key_term, value_term, band_term


def kernel(
    pairs,
    q_ref, k_ref, v_ref, g_ref, pos_ref, bc_ref, bp_ref,
    dq_ref, dk_ref, dv_ref, dp_ref,
    inp, kvp, tab, dqv, dkv0, dkv1, dkv1r, dkvo, band, band16, corer, ysend, yr, xsum, xsend, xr, zsend, zr, xg,
    in_sem, kv_s, kv_r, z_s, z_r, y_s, y_r, c_s, c_r, b_s, b_r, bc_s, bc_r, by_s, by_r, bx_s, bx_r, bz_s, bz_r,
    xg_s, xg_r, out_sem,
):
    groups = pairs // 2
    dp, blk = lax.axis_index("dp"), lax.axis_index("blk")
    x, zl = dp // ZL, dp % ZL
    y, zh, c = blk // 4, (blk // 2) % 2, blk % 2
    z = zh * ZL + zl
    count = 4 * NY

    def at(x_, y_, z_, c_):
        return (x_ * ZL + z_ % ZL, (y_ * 2 + z_ // ZL) * 2 + c_)

    following, before = (dp, (blk + 1) % count), (dp, (blk + count - 1) % count)
    partner = at(x, y, z, 1 - c)
    opposite = (dp, (y * 2 + 1 - zh) * 2 + c)
    y_peers = [at(x, (y + d) % NY, z, c) for d in range(1, NY)]
    x_peers = [at((x + d) % NX, y, z, c) for d in range(1, NX)]
    z_peers = [at(x, y, (z + d) % NZ, c) for d in range(1, NZ)]

    def remote(src, dst, send, recv, device):
        return pltpu.make_async_remote_copy(
            src_ref=src, dst_ref=dst, send_sem=send, recv_sem=recv, device_id=device, device_id_type=MESH
        )

    def wait_bytes(ref, sem):
        pltpu.make_async_copy(ref, ref, sem).wait()

    def cols(p):
        return pl.ds(p * LANES, LANES)

    barrier = pltpu.get_barrier_semaphore()
    peers = [following, before] + y_peers + x_peers + z_peers
    for peer in peers:
        pl.semaphore_signal(barrier, inc=1, device_id=peer, device_id_type=MESH)
    for p in range(pairs):
        for n, ref in ((QUERY, q_ref), (GRAD, g_ref), (KEY, k_ref), (VALUE, v_ref)):
            pltpu.make_async_copy(ref.at[0, :, cols(p)], inp.at[p, n], in_sem.at[p]).start()

    flip = (
        lax.broadcasted_iota(jnp.int32, (16, 16), 0) + lax.broadcasted_iota(jnp.int32, (16, 16), 1) == 15
    )
    turned = jnp.dot(
        jnp.where(flip, 1.0, 0.0).astype(BF16), pos_ref[...], preferred_element_type=F32
    ).astype(BF16)
    sy, sz, sc = NY - 1 - y, 1 - zh, 1 - c
    for p in range(pairs):
        tab[p, sy, sz, sc] = turned[:, p * LANES : (p + 1) * LANES]
    pl.semaphore_wait(barrier, len(peers))

    def shard(g, z_):
        return tab.at[pl.ds(2 * g, 2), sy, z_, sc]

    for g in range(groups):
        remote(shard(g, sz), shard(g, sz), z_s, z_r.at[g], opposite).start()
        for peer in y_peers:
            remote(shard(g, sz), shard(g, sz), y_s, y_r.at[g], peer).start()
        for p in (2 * g, 2 * g + 1):
            for n, ref in ((0, k_ref), (1, v_ref)):
                remote(ref.at[0, :, cols(p)], kvp.at[p, n], kv_s, kv_r.at[p], following).start()
    for g in range(groups):
        wait_bytes(shard(g, 1 - sz), z_r.at[g])
        for peer in y_peers:
            remote(shard(g, 1 - sz), shard(g, 1 - sz), y_s, y_r.at[g], peer).start()

    def share_table(g):
        wait_bytes(tab.at[pl.ds(2 * g, 2), pl.ds(0, NY - 1), :, 0], y_r.at[g])
        mine = tab.at[pl.ds(2 * g, 2), :, :, sc]
        remote(mine, mine, c_s, c_r.at[g], partner).start()

    def pair_step(p):
        wait_bytes(inp.at[p], in_sem.at[p])
        wait_bytes(kvp.at[p], kv_r.at[p])
        keys = jnp.concatenate([inp[p, KEY], kvp[p, 0]], axis=0)
        values = jnp.concatenate([inp[p, VALUE], kvp[p, 1]], axis=0)
        table = tab[p].reshape(32 * 16, LANES)
        lanes = slice(p * LANES, (p + 1) * LANES)
        dq, dk, dv, db = pair_grads(
            inp[p, QUERY], inp[p, GRAD], keys, values, table, bc_ref[:, lanes], bp_ref[:, lanes]
        )
        dqv[p] = dq.astype(BF16)
        pltpu.make_async_copy(dqv.at[p], dq_ref.at[0, :, cols(p)], out_sem).start()
        dkv0[p, 0] = dk[:FRAMES]
        dkv0[p, 1] = dv[:FRAMES]
        dkv1[p, 0] = dk[FRAMES:].astype(BF16)
        dkv1[p, 1] = dv[FRAMES:].astype(BF16)
        db = db.reshape(NY, 2, 2, 16, LANES)
        band[p] = db
        band16[p] = db.astype(BF16)

    def send_back(g):
        two = pl.ds(2 * g, 2)
        remote(band16.at[two, :, :, c], corer.at[two], bc_s, bc_r.at[g], partner).start()
        for p in (2 * g, 2 * g + 1):
            remote(dkv1.at[p], dkv1r.at[p], b_s, b_r.at[p], before).start()

    def chip_sum(g):
        two = pl.ds(2 * g, 2)
        wait_bytes(corer.at[two], bc_r.at[g])
        for p in (2 * g, 2 * g + 1):
            total = band[p, :, :, sc] + corer[p].astype(F32)
            ysend[p] = total.astype(BF16)
        for d, peer in enumerate(y_peers):
            sink = NY - 1 - (y + d + 1) % NY
            remote(ysend.at[two, sink], yr.at[d, two], by_s, by_r.at[g], peer).start()

    def y_sum(g):
        two = pl.ds(2 * g, 2)
        wait_bytes(yr.at[:, two], by_r.at[g])
        for p in (2 * g, 2 * g + 1):
            total = band[p, sy, :, sc] + corer[p, sy].astype(F32)
            for d in range(NY - 1):
                total = total + yr[d, p].astype(F32)
            xsum[p] = total
            xsend[p] = total.astype(BF16)

        @pl.when(x != g)
        def _():
            slot = (x + NX - g) % NX - 1
            remote(xsend.at[two], xr.at[slot], bx_s.at[g], bx_r, at(g, y, z, c)).start()

    share_table(0)
    for g in range(groups):
        wait_bytes(tab.at[pl.ds(2 * g, 2), :, :, 0], c_r.at[g])
        pair_step(2 * g)
        if g + 1 < groups:
            share_table(g + 1)
        pair_step(2 * g + 1)
        send_back(g)
        if g >= 1:
            chip_sum(g - 1)
        if g >= 2:
            y_sum(g - 2)
    chip_sum(groups - 1)
    y_sum(groups - 2)

    def finish_keys(p):
        wait_bytes(dkv1r.at[p], b_r.at[p])
        dkvo[p] = (dkv0[p] + dkv1r[p].astype(F32)).astype(BF16)
        pltpu.make_async_copy(dkvo.at[p, 0], dk_ref.at[0, :, cols(p)], out_sem).start()
        pltpu.make_async_copy(dkvo.at[p, 1], dv_ref.at[0, :, cols(p)], out_sem).start()

    y_sum(groups - 1)

    mine = pl.ds(2 * x, 2)
    wait_bytes(xr, bx_r)
    total = xsum[mine]
    for d in range(NX - 1):
        total = total + xr[d].astype(F32)
    zsend[...] = total.astype(BF16)
    xsum[mine] = total
    for d, peer in enumerate(z_peers):
        half = (z + d + 1) % NZ // ZL
        remote(zsend.at[:, 1 - half], zr.at[d], bz_s, bz_r, peer).start()
    for p in range(pairs):
        finish_keys(p)
    wait_bytes(zr, bz_r)
    total = xsum[mine, sz]
    for d in range(NZ - 1):
        total = total + zr[d].astype(F32)
    xg[x] = total
    for peer in x_peers:
        remote(xg.at[x], xg.at[x], xg_s, xg_r, peer).start()
    wait_bytes(xg.at[pl.ds(0, NX - 1)], xg_r)
    for p in range(pairs):
        rows = xg[p // 2, p % 2]
        for r in range(16):
            dp_ref[15 - r : 16 - r, p * LANES : (p + 1) * LANES] = rows[r : r + 1]

    wait_bytes(kvp, kv_s)
    wait_bytes(tab.at[:, 0, 0, 0], z_s)
    wait_bytes(tab.at[:, pl.ds(0, NY - 1), :, 0], y_s)
    wait_bytes(tab.at[:, :, :, 0], c_s)
    wait_bytes(dkv1, b_s)
    wait_bytes(corer, bc_s)
    wait_bytes(yr, by_s)
    for g in range(groups):

        @pl.when(x != g)
        def _():
            wait_bytes(xr.at[0], bx_s.at[g])

    wait_bytes(zr, bz_s)
    wait_bytes(xg.at[pl.ds(0, NX - 1)], xg_s)
    wait_bytes(inp.at[:, pl.ds(0, 3)], out_sem)


def local(query_rows, key_rows, value_rows, grad_out, pos_keys, bias_content, bias_position):
    width = query_rows.shape[2]
    pairs = width // LANES
    groups = pairs // 2
    rows = query_rows.shape
    sem = pltpu.SemaphoreType.DMA
    hbm = pl.BlockSpec(memory_space=pl.ANY)
    vmem = pl.BlockSpec(memory_space=pltpu.VMEM)
    tile = (FRAMES, LANES)
    small = (16, LANES)
    scratch = [
        pltpu.VMEM((pairs, 4, *tile), BF16),
        pltpu.VMEM((pairs, 2, *tile), BF16),
        pltpu.VMEM((pairs, NY, 2, 2, *small), BF16),
        pltpu.VMEM((pairs, *tile), BF16),
        pltpu.VMEM((pairs, 2, *tile), F32),
        pltpu.VMEM((pairs, 2, *tile), BF16),
        pltpu.VMEM((pairs, 2, *tile), BF16),
        pltpu.VMEM((pairs, 2, *tile), BF16),
        pltpu.VMEM((pairs, NY, 2, 2, *small), F32),
        pltpu.VMEM((pairs, NY, 2, 2, *small), BF16),
        pltpu.VMEM((pairs, NY, 2, *small), BF16),
        pltpu.VMEM((pairs, NY, 2, *small), BF16),
        pltpu.VMEM((NY - 1, pairs, 2, *small), BF16),
        pltpu.VMEM((pairs, 2, *small), F32),
        pltpu.VMEM((pairs, 2, *small), BF16),
        pltpu.VMEM((NX - 1, 2, 2, *small), BF16),
        pltpu.VMEM((2, 2, *small), BF16),
        pltpu.VMEM((NZ - 1, 2, *small), BF16),
        pltpu.VMEM((NX, 2, *small), F32),
        sem((pairs,)),
        sem, sem((pairs,)),
        sem, sem((groups,)),
        sem, sem((groups,)),
        sem, sem((groups,)),
        sem, sem((pairs,)),
        sem, sem((groups,)),
        sem, sem((groups,)),
        sem((groups,)), sem,
        sem, sem,
        sem, sem,
        sem,
    ]
    return pl.pallas_call(
        functools.partial(kernel, pairs),
        out_shape=(
            jax.ShapeDtypeStruct(rows, BF16),
            jax.ShapeDtypeStruct(rows, BF16),
            jax.ShapeDtypeStruct(rows, BF16),
            jax.ShapeDtypeStruct((16, width), F32),
        ),
        in_specs=[hbm, hbm, hbm, hbm, vmem, vmem, vmem],
        out_specs=(hbm, hbm, hbm, vmem),
        scratch_shapes=scratch,
        compiler_params=pltpu.CompilerParams(collective_id=0, has_side_effects=True, vmem_limit_bytes=48 << 20),
    )(
        query_rows, key_rows, value_rows, grad_out, pos_keys,
        bias_content.reshape(1, width), bias_position.reshape(1, width),
    )


def solution(mesh):
    wide = P("dp", "blk", None)
    return jax.shard_map(
        local,
        mesh=mesh,
        in_specs=(wide, wide, wide, wide, P("blk", None), P(), P()),
        out_specs=(wide, wide, wide, P("blk", None)),
        check_vma=False,
    )
```

```python
import functools

import jax
import jax.numpy as jnp
from jax import lax
from jax.experimental import pallas as pl
from jax.experimental.pallas import tpu as pltpu
from jax.sharding import PartitionSpec as P

MESH = pl.DeviceIdType.MESH
DH = 64
LANES = 2 * DH
FRAMES = 128
F32, BF16 = jnp.float32, jnp.bfloat16
NX, NY, NZ, ZL = 4, 8, 8, 4
QUERY, GRAD, KEY, VALUE = range(4)
GATHER = ((0, 1), (1, 1), (2, 2), (4, 2), (6, 2))
REDUCE = ((0, 2), (2, 2), (4, 2), (6, 1), (7, 1))


def contract_lanes(a, b):
    return lax.dot_general(a, b, (((1,), (1,)), ((), ())), preferred_element_type=F32)


def contract_rows(a, b):
    return lax.dot_general(a, b, (((0,), (0,)), ((), ())), preferred_element_type=F32)


def place_roll(x):
    rows = x.shape[0]
    blocks = [
        pltpu.roll(x[8 * a : 8 * a + 8], (127 - 8 * a) % 128, 1) for a in range(rows // 8)
    ]
    x = jnp.concatenate(blocks, axis=0)
    row = lax.broadcasted_iota(jnp.int32, x.shape, 0)
    for bit in range(3):
        moved = pltpu.roll(x, 128 - 2**bit, 1)
        x = jnp.where(((row >> bit) & 1) == 1, moved, x)
    return x


def pair_grads(q, grad, keys, values, table, bias_c, bias_p):
    first = lax.broadcasted_iota(jnp.int32, (FRAMES, LANES), 1) < DH

    def stacked(x):
        zero = jnp.zeros_like(x)
        both = jnp.concatenate([jnp.where(first, x, zero), jnp.where(first, zero, x)], axis=0)
        return both.astype(BF16)

    q32 = q.astype(F32)
    content_in = stacked(q32 + bias_c)
    position_in = stacked(q32 + bias_p)
    grad_in = stacked(grad.astype(F32))
    content = contract_lanes(content_in, keys)
    spread = contract_lanes(position_in, table)
    weights = contract_lanes(grad_in, values)
    shape = (2 * FRAMES, FRAMES)
    frame = lax.broadcasted_iota(jnp.int32, shape, 0) & (FRAMES - 1)
    upper = lax.broadcasted_iota(jnp.int32, shape, 1) + frame >= FRAMES - 1

    def select(at):
        picked = jnp.where(upper, spread[:, at : at + 128], spread[:, at + 128 : at + 256])
        return pltpu.roll(picked, 1, 1, stride=1, stride_axis=0)

    factor = DH**-0.5
    s0 = (content[:, :128] + select(256)) * factor
    s1 = (content[:, 128:] + select(0)) * factor
    top = jnp.max(jnp.maximum(s0, s1), axis=1, keepdims=True)
    e0, e1 = jnp.exp(s0 - top), jnp.exp(s1 - top)
    inverse = 1.0 / jnp.sum(e0 + e1, axis=1, keepdims=True)
    a0, a1 = e0 * inverse, e1 * inverse
    w0, w1 = weights[:, :128], weights[:, 128:]
    delta = jnp.sum(a0 * w0 + a1 * w1, axis=1, keepdims=True)
    d0 = a0 * (w0 - delta) * factor
    d1 = a1 * (w1 - delta) * factor
    dscore = jnp.concatenate([d0, d1], axis=1).astype(BF16)
    attention = jnp.concatenate([a0, a1], axis=1).astype(BF16)
    p0, p1 = place_roll(d0), place_roll(d1)
    zero = jnp.zeros_like(p0)
    location = jnp.concatenate(
        [
            jnp.where(upper, p1, zero),
            jnp.where(upper, zero, p1),
            jnp.where(upper, p0, zero),
            jnp.where(upper, zero, p0),
        ],
        axis=1,
    ).astype(BF16)
    both = jnp.dot(
        jnp.concatenate([dscore, location], axis=1),
        jnp.concatenate([keys, table], axis=0),
        preferred_element_type=F32,
    )
    query_gradient = jnp.where(first, both[:FRAMES], both[FRAMES:])
    key_term = contract_rows(dscore, content_in)
    value_term = contract_rows(attention, grad_in)
    band_term = contract_rows(location, position_in)
    return query_gradient, key_term, value_term, band_term


def kernel(
    pairs,
    q_ref, k_ref, v_ref, g_ref, pos_ref, bc_ref, bp_ref,
    dq_ref, dk_ref, dv_ref, dp_ref,
    dqv, dkvo, inp, posv, biases, kvp, tab, dkv0, dkv1, dkv1r, band, band16, corer, ysend, yr, xr, zown, zr,
    in_sem, first_sem, kv_s, kv_r, z_s, z_r, y_s, y_r, c_s, c_r, b_s, b_r, bc_s, bc_r, by_s, by_r, bx_s, bx_r, bz_s, bz_r, out_sem,
):
    dp, blk = lax.axis_index("dp"), lax.axis_index("blk")
    x, zl = dp // ZL, dp % ZL
    y, zh, c = blk // 4, (blk // 2) % 2, blk % 2
    z = zh * ZL + zl
    count = 4 * NY

    def at(x_, y_, z_, c_):
        return (x_ * ZL + z_ % ZL, (y_ * 2 + z_ // ZL) * 2 + c_)

    following, before = (dp, (blk + 1) % count), (dp, (blk + count - 1) % count)
    partner = at(x, y, z, 1 - c)
    opposite = (dp, (y * 2 + 1 - zh) * 2 + c)
    y_peers = [at(x, (y + d) % NY, z, c) for d in range(1, NY)]
    x_peers = [at((x + d) % NX, y, z, c) for d in range(1, NX)]
    z_peers = [at(x, y, (z + d) % NZ, c) for d in range(1, NZ)]
    y_order = (3, 2, 4, 1, 5, 0, 6)

    def remote(src, dst, send, recv, device):
        return pltpu.make_async_remote_copy(
            src_ref=src, dst_ref=dst, send_sem=send, recv_sem=recv, device_id=device, device_id_type=MESH
        )

    def wait_bytes(ref, sem):
        pltpu.make_async_copy(ref, ref, sem).wait()

    def cols(p):
        return pl.ds(p * LANES, LANES)

    def chunk(k, chunks):
        return pl.ds(*chunks[k])

    barrier = pltpu.get_barrier_semaphore()
    peers = [following, before] + y_peers + x_peers + z_peers
    for peer in peers:
        pl.semaphore_signal(barrier, inc=1, device_id=peer, device_id_type=MESH)
    pos_copy = pltpu.make_async_copy(pos_ref, posv, first_sem.at[0])
    pos_copy.start()
    bias_copies = [
        pltpu.make_async_copy(ref, biases.at[n], first_sem.at[1 + n]) for n, ref in enumerate((bc_ref, bp_ref))
    ]
    for copy in bias_copies:
        copy.start()
    for p in range(pairs):
        for n, ref in ((QUERY, q_ref), (GRAD, g_ref), (KEY, k_ref), (VALUE, v_ref)):
            pltpu.make_async_copy(ref.at[0, :, cols(p)], inp.at[p, n], in_sem.at[p]).start()

    flip = (
        lax.broadcasted_iota(jnp.int32, (16, 16), 0) + lax.broadcasted_iota(jnp.int32, (16, 16), 1) == 15
    )
    pos_copy.wait()
    turned = jnp.dot(
        jnp.where(flip, 1.0, 0.0).astype(BF16), posv[...], preferred_element_type=F32
    ).astype(BF16)
    sy, sz, sc = NY - 1 - y, 1 - zh, 1 - c
    for p in range(pairs):
        tab[p, sy, sz, sc] = turned[:, p * LANES : (p + 1) * LANES]
    for copy in bias_copies:
        copy.wait()
    pl.semaphore_wait(barrier, len(peers))

    def shard(k, z_):
        return tab.at[chunk(k, GATHER), sy, z_, sc]

    def along_y(k, z_):
        for d in y_order:
            remote(shard(k, z_), shard(k, z_), y_s, y_r.at[k], y_peers[d]).start()

    def shift(k):
        for p in range(GATHER[k][0], sum(GATHER[k])):
            for n, ref in ((0, k_ref), (1, v_ref)):
                remote(ref.at[0, :, cols(p)], kvp.at[p, n], kv_s, kv_r.at[p], following).start()

    chunks = len(GATHER)
    for k in range(chunks):
        remote(shard(k, sz), shard(k, sz), z_s, z_r.at[k], opposite).start()
    for k in range(chunks):
        shift(k)
        if k < chunks - 1:
            along_y(k, sz)
    for k in range(chunks):
        wait_bytes(shard(k, 1 - sz), z_r.at[k])
        along_y(k, 1 - sz)
        if k == 1:
            along_y(chunks - 1, sz)

    def share_table(k):
        wait_bytes(tab.at[chunk(k, GATHER), pl.ds(0, NY - 1), :, 0], y_r.at[k])
        mine = tab.at[chunk(k, GATHER), :, :, sc]
        remote(mine, mine, c_s, c_r.at[k], partner).start()

    def pair_step(p):
        wait_bytes(inp.at[p], in_sem.at[p])
        wait_bytes(kvp.at[p], kv_r.at[p])
        keys = jnp.concatenate([inp[p, KEY], kvp[p, 0]], axis=0)
        values = jnp.concatenate([inp[p, VALUE], kvp[p, 1]], axis=0)
        table = tab[p].reshape(32 * 16, LANES)
        lanes = slice(p * LANES, (p + 1) * LANES)
        dq, dk, dv, db = pair_grads(
            inp[p, QUERY], inp[p, GRAD], keys, values, table, biases[0, :, lanes], biases[1, :, lanes]
        )
        dqv[p] = dq.astype(BF16)
        pltpu.make_async_copy(dqv.at[p], dq_ref.at[0, :, cols(p)], out_sem.at[0]).start()
        dkv0[p, 0] = dk[:FRAMES]
        dkv0[p, 1] = dv[:FRAMES]
        dkv1[p, 0] = dk[FRAMES:].astype(BF16)
        dkv1[p, 1] = dv[FRAMES:].astype(BF16)
        db = db.reshape(NY, 2, 2, 16, LANES)
        band[p] = db
        band16[p] = db.astype(BF16)

    def send_back(k):
        part = chunk(k, REDUCE)
        remote(band16.at[part, :, :, c], corer.at[part], bc_s, bc_r.at[k], partner).start()
        for p in range(REDUCE[k][0], sum(REDUCE[k])):
            remote(dkv1.at[p], dkv1r.at[p], b_s, b_r.at[p], before).start()

    def chip_sum(k):
        part = chunk(k, REDUCE)
        wait_bytes(corer.at[part], bc_r.at[k])
        for p in range(REDUCE[k][0], sum(REDUCE[k])):
            total = band[p, :, :, sc] + corer[p].astype(F32)
            ysend[p] = total.astype(BF16)
        for d in y_order:
            sink = NY - 1 - (y + d + 1) % NY
            remote(ysend.at[part, sink], yr.at[d, part], by_s, by_r.at[k], y_peers[d]).start()

    def y_sum(k):
        part = chunk(k, REDUCE)
        wait_bytes(yr.at[:, part], by_r.at[k])
        for p in range(REDUCE[k][0], sum(REDUCE[k])):
            total = band[p, sy, :, sc] + corer[p, sy].astype(F32)
            for d in range(NY - 1):
                total = total + yr[d, p].astype(F32)
            xr[x, p] = total.astype(BF16)
        for peer in x_peers:
            remote(xr.at[x, part], xr.at[x, part], bx_s, bx_r.at[k], peer).start()

    def x_sum(k):
        part = chunk(k, REDUCE)
        wait_bytes(xr.at[pl.ds(0, NX - 1), part], bx_r.at[k])
        for p in range(REDUCE[k][0], sum(REDUCE[k])):
            total = xr[0, p].astype(F32)
            for d in range(1, NX):
                total = total + xr[d, p].astype(F32)
            zown[p] = total.astype(BF16)
            zr[z, p] = zown[p, sz]
        for d, peer in enumerate(z_peers):
            half = (z + d + 1) % NZ // ZL
            remote(zown.at[part, 1 - half], zr.at[z, part], bz_s, bz_r, peer).start()

    def finish_keys(p):
        wait_bytes(dkv1r.at[p], b_r.at[p])
        dkvo[p] = (dkv0[p] + dkv1r[p].astype(F32)).astype(BF16)
        for n, ref in ((0, dk_ref), (1, dv_ref)):
            pltpu.make_async_copy(dkvo.at[p, n], ref.at[0, :, cols(p)], out_sem.at[1]).start()

    done = 0
    share_table(0)
    for k, (start, number) in enumerate(GATHER):
        wait_bytes(tab.at[chunk(k, GATHER), :, :, 0], c_r.at[k])
        for p in range(start, start + number):
            pair_step(p)
            if p == start and k + 1 < chunks:
                share_table(k + 1)
            if p + 1 == sum(REDUCE[done]):
                send_back(done)
                if done >= 1:
                    chip_sum(done - 1)
                done += 1
    last = len(REDUCE) - 1
    y_sum(0)
    chip_sum(last)
    for k in range(1, last):
        y_sum(k)
        x_sum(k - 1)
    for p in range(pairs - 2):
        finish_keys(p)
    y_sum(last)
    x_sum(last - 1)
    x_sum(last)
    for p in range(pairs - 2, pairs):
        finish_keys(p)
    wait_bytes(zr.at[pl.ds(0, NZ - 1)], bz_r)
    for p in range(pairs):
        total = zr[0, p].astype(F32)
        for d in range(1, NZ):
            total = total + zr[d, p].astype(F32)
        for r in range(16):
            dp_ref[15 - r : 16 - r, p * LANES : (p + 1) * LANES] = total[r : r + 1]

    wait_bytes(kvp, kv_s)
    wait_bytes(tab.at[:, 0, 0, 0], z_s)
    wait_bytes(tab.at[:, pl.ds(0, NY - 1), :, 0], y_s)
    wait_bytes(tab.at[:, :, :, 0], c_s)
    wait_bytes(dkv1, b_s)
    wait_bytes(corer, bc_s)
    wait_bytes(yr, by_s)
    wait_bytes(xr.at[pl.ds(0, NX - 1)], bx_s)
    wait_bytes(zr.at[pl.ds(0, NZ - 1)], bz_s)
    wait_bytes(dqv, out_sem.at[0])
    wait_bytes(dkvo, out_sem.at[1])


def write_out(*refs):
    sources, results, held, sems = refs[:4], refs[4:8], refs[8:12], refs[12]
    loads = [pltpu.make_async_copy(a, b, sems.at[0, n]) for n, (a, b) in enumerate(zip(sources, held))]
    stores = [pltpu.make_async_copy(a, b, sems.at[1, n]) for n, (a, b) in enumerate(zip(held, results))]
    for copy in loads:
        copy.start()
    for load, store in zip(loads, stores):
        load.wait()
        store.start()
    for copy in stores:
        copy.wait()


def local(query_rows, key_rows, value_rows, grad_out, pos_keys, bias_content, bias_position):
    width = query_rows.shape[2]
    pairs = width // LANES
    rows = query_rows.shape
    sem = pltpu.SemaphoreType.DMA
    hbm = pl.BlockSpec(memory_space=pltpu.HBM)
    vmem = pl.BlockSpec(memory_space=pltpu.VMEM)
    tile = (FRAMES, LANES)
    small = (16, LANES)
    gather, reduce = sem((len(GATHER),)), sem((len(REDUCE),))
    scratch = [
        pltpu.VMEM((pairs, *tile), BF16),
        pltpu.VMEM((pairs, 2, *tile), BF16),
        pltpu.VMEM((pairs, 4, *tile), BF16),
        pltpu.VMEM((16, width), BF16),
        pltpu.VMEM((2, 1, width), F32),
        pltpu.VMEM((pairs, 2, *tile), BF16),
        pltpu.VMEM((pairs, NY, 2, 2, *small), BF16),
        pltpu.VMEM((pairs, 2, *tile), F32),
        pltpu.VMEM((pairs, 2, *tile), BF16),
        pltpu.VMEM((pairs, 2, *tile), BF16),
        pltpu.VMEM((pairs, NY, 2, 2, *small), F32),
        pltpu.VMEM((pairs, NY, 2, 2, *small), BF16),
        pltpu.VMEM((pairs, NY, 2, *small), BF16),
        pltpu.VMEM((pairs, NY, 2, *small), BF16),
        pltpu.VMEM((NY - 1, pairs, 2, *small), BF16),
        pltpu.VMEM((NX, pairs, 2, *small), BF16),
        pltpu.VMEM((pairs, 2, *small), BF16),
        pltpu.VMEM((NZ, pairs, *small), BF16),
        sem((pairs,)),
        sem((3,)),
        sem, sem((pairs,)),
        sem, gather,
        sem, gather,
        sem, gather,
        sem, sem((pairs,)),
        sem, reduce,
        sem, reduce,
        sem, reduce,
        sem, sem,
        sem((2,)),
    ]
    wide = jax.ShapeDtypeStruct(rows, BF16)
    results = (wide, wide, wide, jax.ShapeDtypeStruct((16, width), F32))
    raw = pl.pallas_call(
        functools.partial(kernel, pairs),
        out_shape=results,
        in_specs=[hbm] * 7,
        out_specs=(hbm, hbm, hbm, vmem),
        scratch_shapes=scratch,
        compiler_params=pltpu.CompilerParams(
            collective_id=0, has_side_effects=True, vmem_limit_bytes=67_043_328
        ),
    )(
        query_rows, key_rows, value_rows, grad_out, pos_keys,
        bias_content.reshape(1, width), bias_position.reshape(1, width),
    )
    return pl.pallas_call(
        write_out,
        out_shape=results,
        in_specs=[hbm] * 4,
        out_specs=(hbm,) * 4,
        scratch_shapes=[pltpu.VMEM(a.shape, a.dtype) for a in results] + [sem((2, 4))],
        compiler_params=pltpu.CompilerParams(vmem_limit_bytes=67_043_328),
    )(*raw)


def solution(mesh):
    wide = P("dp", "blk", None)
    return jax.shard_map(
        local,
        mesh=mesh,
        in_specs=(wide, wide, wide, wide, P("blk", None), P(), P()),
        out_specs=(wide, wide, wide, P("blk", None)),
        check_vma=False,
    )
```

```python
import functools

import jax
import jax.numpy as jnp
from jax import lax
from jax.experimental import pallas as pl
from jax.experimental.pallas import tpu as pltpu
from jax.sharding import PartitionSpec as P

MESH = pl.DeviceIdType.MESH
DH = 64
LANES = 2 * DH
FRAMES = 128
F32, BF16 = jnp.float32, jnp.bfloat16
NX, NY, NZ, ZL = 4, 8, 8, 4
QUERY, GRAD, KEY, VALUE = range(4)
GATHER = ((0, 1), (1, 1), (2, 2), (4, 2), (6, 2))
REDUCE = ((0, 2), (2, 2), (4, 2), (6, 1), (7, 1))


def contract_lanes(a, b):
    return lax.dot_general(a, b, (((1,), (1,)), ((), ())), preferred_element_type=F32)


def contract_rows(a, b):
    return lax.dot_general(a, b, (((0,), (0,)), ((), ())), preferred_element_type=F32)


def place_roll(d):
    rows = d.shape[0]
    shape = (FRAMES, FRAMES)
    flip = lax.broadcasted_iota(jnp.int32, shape, 0) + lax.broadcasted_iota(jnp.int32, shape, 1) == FRAMES - 1
    flip = jnp.where(flip, 1.0, 0.0).astype(BF16)

    def turned(m):
        return jnp.concatenate(
            [jnp.dot(flip, m[at : at + FRAMES], preferred_element_type=F32) for at in range(0, rows, FRAMES)], axis=0
        )

    upside = turned(d)
    rolled = [pltpu.roll(upside[:, at : at + FRAMES], 0, 1, stride=1, stride_axis=0) for at in (0, FRAMES)]
    placed = turned(jnp.concatenate(rolled, axis=1).astype(BF16)).astype(BF16)
    return placed[:, :FRAMES], placed[:, FRAMES:]


def pair_grads(q, grad, keys, values, table, bias_c, bias_p):
    first = lax.broadcasted_iota(jnp.int32, (FRAMES, LANES), 1) < DH

    def stacked(x):
        zero = jnp.zeros_like(x)
        both = jnp.concatenate([jnp.where(first, x, zero), jnp.where(first, zero, x)], axis=0)
        return both.astype(BF16)

    q32 = q.astype(F32)
    content_in = stacked(q32 + bias_c)
    position_in = stacked(q32 + bias_p)
    grad_in = stacked(grad.astype(F32))
    content = contract_lanes(content_in, keys)
    spread = contract_lanes(position_in, table)
    weights = contract_lanes(grad_in, values)
    shape = (2 * FRAMES, FRAMES)
    frame = lax.broadcasted_iota(jnp.int32, shape, 0) & (FRAMES - 1)
    upper = lax.broadcasted_iota(jnp.int32, shape, 1) + frame >= FRAMES - 1

    def select(at):
        picked = jnp.where(upper, spread[:, at : at + 128], spread[:, at + 128 : at + 256])
        return pltpu.roll(picked, 1, 1, stride=1, stride_axis=0)

    factor = DH**-0.5
    s0 = (content[:, :128] + select(256)) * factor
    s1 = (content[:, 128:] + select(0)) * factor
    top = jnp.max(jnp.maximum(s0, s1), axis=1, keepdims=True)
    e0, e1 = jnp.exp(s0 - top), jnp.exp(s1 - top)
    inverse = 1.0 / jnp.sum(e0 + e1, axis=1, keepdims=True)
    a0, a1 = e0 * inverse, e1 * inverse
    w0, w1 = weights[:, :128], weights[:, 128:]
    delta = jnp.sum(a0 * w0 + a1 * w1, axis=1, keepdims=True)
    d0 = a0 * (w0 - delta) * factor
    d1 = a1 * (w1 - delta) * factor
    dscore = jnp.concatenate([d0, d1], axis=1).astype(BF16)
    attention = jnp.concatenate([a0, a1], axis=1).astype(BF16)
    p0, p1 = place_roll(dscore)
    zero = jnp.zeros_like(p0)
    location = jnp.concatenate(
        [
            jnp.where(upper, p1, zero),
            jnp.where(upper, zero, p1),
            jnp.where(upper, p0, zero),
            jnp.where(upper, zero, p0),
        ],
        axis=1,
    )
    both = jnp.dot(
        jnp.concatenate([dscore, location], axis=1),
        jnp.concatenate([keys, table], axis=0),
        preferred_element_type=F32,
    )
    query_gradient = jnp.where(first, both[:FRAMES], both[FRAMES:])
    key_term = contract_rows(dscore, content_in)
    value_term = contract_rows(attention, grad_in)
    band_term = contract_rows(location, position_in)
    return query_gradient, key_term, value_term, band_term


def kernel(
    pairs,
    q_ref, k_ref, v_ref, g_ref, pos_ref, bc_ref, bp_ref,
    dq_ref, dk_ref, dv_ref, dp_ref,
    dqv, dkvo, inp, posv, biases, kvp, tab, dkv0, dkv1, dkv1r, band, band16, corer, ysend, yr, xr, zown, zr,
    in_sem, first_sem, kv_s, kv_r, z_s, z_r, y_s, y_r, c_s, c_r, b_s, b_r, bc_s, bc_r, by_s, by_r, bx_s, bx_r, bz_s, bz_r, out_sem,
):
    dp, blk = lax.axis_index("dp"), lax.axis_index("blk")
    x, zl = dp // ZL, dp % ZL
    y, zh, c = blk // 4, (blk // 2) % 2, blk % 2
    z = zh * ZL + zl
    count = 4 * NY

    def at(x_, y_, z_, c_):
        return (x_ * ZL + z_ % ZL, (y_ * 2 + z_ // ZL) * 2 + c_)

    following, before = (dp, (blk + 1) % count), (dp, (blk + count - 1) % count)
    partner = at(x, y, z, 1 - c)
    opposite = (dp, (y * 2 + 1 - zh) * 2 + c)
    y_peers = [at(x, (y + d) % NY, z, c) for d in range(1, NY)]
    x_peers = [at((x + d) % NX, y, z, c) for d in range(1, NX)]
    z_peers = [at(x, y, (z + d) % NZ, c) for d in range(1, NZ)]
    y_order = (3, 2, 4, 1, 5, 0, 6)

    def remote(src, dst, send, recv, device):
        return pltpu.make_async_remote_copy(
            src_ref=src, dst_ref=dst, send_sem=send, recv_sem=recv, device_id=device, device_id_type=MESH
        )

    def wait_bytes(ref, sem):
        pltpu.make_async_copy(ref, ref, sem).wait()

    def cols(p):
        return pl.ds(p * LANES, LANES)

    def chunk(k, chunks):
        return pl.ds(*chunks[k])

    barrier = pltpu.get_barrier_semaphore()
    peers = [following, before] + y_peers + x_peers + z_peers
    for peer in peers:
        pl.semaphore_signal(barrier, inc=1, device_id=peer, device_id_type=MESH)
    pos_copy = pltpu.make_async_copy(pos_ref, posv, first_sem.at[0])
    pos_copy.start()
    bias_copies = [
        pltpu.make_async_copy(ref, biases.at[n], first_sem.at[1 + n]) for n, ref in enumerate((bc_ref, bp_ref))
    ]
    for copy in bias_copies:
        copy.start()

    flip = (
        lax.broadcasted_iota(jnp.int32, (16, 16), 0) + lax.broadcasted_iota(jnp.int32, (16, 16), 1) == 15
    )
    pos_copy.wait()
    turned = jnp.dot(
        jnp.where(flip, 1.0, 0.0).astype(BF16), posv[...], preferred_element_type=F32
    ).astype(BF16)
    sy, sz, sc = NY - 1 - y, 1 - zh, 1 - c
    for p in range(pairs):
        tab[p, sy, sz, sc] = turned[:, p * LANES : (p + 1) * LANES]
    for copy in bias_copies:
        copy.wait()
    pl.semaphore_wait(barrier, len(peers))

    def shard(k, z_):
        return tab.at[chunk(k, GATHER), sy, z_, sc]

    def along_y(k, z_):
        for d in y_order:
            remote(shard(k, z_), shard(k, z_), y_s, y_r.at[k], y_peers[d]).start()

    def shift(k):
        for p in range(GATHER[k][0], sum(GATHER[k])):
            for n, ref in ((0, k_ref), (1, v_ref)):
                remote(ref.at[0, :, cols(p)], kvp.at[p, n], kv_s, kv_r.at[p], following).start()

    chunks = len(GATHER)

    def pass_on(k):
        wait_bytes(shard(k, 1 - sz), z_r.at[k])
        along_y(k, 1 - sz)

    for k in range(chunks):
        remote(shard(k, sz), shard(k, sz), z_s, z_r.at[k], opposite).start()
    for k in (0, 1):
        along_y(k, sz)
        shift(k)
    along_y(2, sz)
    for p in range(pairs):
        for n, ref in ((QUERY, q_ref), (GRAD, g_ref), (KEY, k_ref), (VALUE, v_ref)):
            pltpu.make_async_copy(ref.at[0, :, cols(p)], inp.at[p, n], in_sem.at[p]).start()
    pass_on(0)
    pass_on(1)
    shift(2)
    pass_on(2)
    along_y(3, sz)
    shift(3)

    def share_table(k):
        wait_bytes(tab.at[chunk(k, GATHER), pl.ds(0, NY - 1), :, 0], y_r.at[k])
        mine = tab.at[chunk(k, GATHER), :, :, sc]
        remote(mine, mine, c_s, c_r.at[k], partner).start()

    def pair_step(p):
        wait_bytes(inp.at[p], in_sem.at[p])
        wait_bytes(kvp.at[p], kv_r.at[p])
        keys = jnp.concatenate([inp[p, KEY], kvp[p, 0]], axis=0)
        values = jnp.concatenate([inp[p, VALUE], kvp[p, 1]], axis=0)
        table = tab[p].reshape(32 * 16, LANES)
        lanes = slice(p * LANES, (p + 1) * LANES)
        dq, dk, dv, db = pair_grads(
            inp[p, QUERY], inp[p, GRAD], keys, values, table, biases[0, :, lanes], biases[1, :, lanes]
        )
        dqv[p] = dq.astype(BF16)
        pltpu.make_async_copy(dqv.at[p], dq_ref.at[0, :, cols(p)], out_sem.at[0]).start()
        dkv0[p, 0] = dk[:FRAMES]
        dkv0[p, 1] = dv[:FRAMES]
        dkv1[p, 0] = dk[FRAMES:].astype(BF16)
        dkv1[p, 1] = dv[FRAMES:].astype(BF16)
        db = db.reshape(NY, 2, 2, 16, LANES)
        band[p] = db
        band16[p] = db.astype(BF16)

    def send_back(k):
        part = chunk(k, REDUCE)
        remote(band16.at[part, :, :, c], corer.at[part], bc_s, bc_r.at[k], partner).start()
        for p in range(REDUCE[k][0], sum(REDUCE[k])):
            remote(dkv1.at[p], dkv1r.at[p], b_s, b_r.at[p], before).start()

    def chip_sum(k):
        part = chunk(k, REDUCE)
        wait_bytes(corer.at[part], bc_r.at[k])
        for p in range(REDUCE[k][0], sum(REDUCE[k])):
            total = band[p, :, :, sc] + corer[p].astype(F32)
            ysend[p] = total.astype(BF16)
        for d in y_order:
            sink = NY - 1 - (y + d + 1) % NY
            remote(ysend.at[part, sink], yr.at[d, part], by_s, by_r.at[k], y_peers[d]).start()

    def y_sum(k):
        part = chunk(k, REDUCE)
        wait_bytes(yr.at[:, part], by_r.at[k])
        for p in range(REDUCE[k][0], sum(REDUCE[k])):
            total = band[p, sy, :, sc] + corer[p, sy].astype(F32)
            for d in range(NY - 1):
                total = total + yr[d, p].astype(F32)
            xr[x, p] = total.astype(BF16)
        for peer in x_peers:
            remote(xr.at[x, part], xr.at[x, part], bx_s, bx_r.at[k], peer).start()

    def x_sum(k):
        part = chunk(k, REDUCE)
        wait_bytes(xr.at[pl.ds(0, NX - 1), part], bx_r.at[k])
        for p in range(REDUCE[k][0], sum(REDUCE[k])):
            total = xr[0, p].astype(F32)
            for d in range(1, NX):
                total = total + xr[d, p].astype(F32)
            zown[p] = total.astype(BF16)
            zr[z, p] = zown[p, sz]
        for d, peer in enumerate(z_peers):
            half = (z + d + 1) % NZ // ZL
            remote(zown.at[part, 1 - half], zr.at[z, part], bz_s, bz_r, peer).start()

    def finish_keys(p):
        wait_bytes(dkv1r.at[p], b_r.at[p])
        dkvo[p] = (dkv0[p] + dkv1r[p].astype(F32)).astype(BF16)
        for n, ref in ((0, dk_ref), (1, dv_ref)):
            pltpu.make_async_copy(dkvo.at[p, n], ref.at[0, :, cols(p)], out_sem.at[1]).start()

    done = 0
    share_table(0)
    pass_on(3)
    share_table(1)
    along_y(4, sz)
    pass_on(4)
    shift(4)
    for k, (start, number) in enumerate(GATHER):
        wait_bytes(tab.at[chunk(k, GATHER), :, :, 0], c_r.at[k])
        for p in range(start, start + number):
            pair_step(p)
            if p == start and k + 2 < chunks:
                share_table(k + 2)
            if p + 1 == sum(REDUCE[done]):
                send_back(done)
                if done >= 1:
                    chip_sum(done - 1)
                done += 1
    last = len(REDUCE) - 1
    y_sum(0)
    chip_sum(last)
    y_sum(1)
    x_sum(0)
    y_sum(2)
    y_sum(3)
    x_sum(1)
    y_sum(last)
    x_sum(2)
    x_sum(3)
    for p in range(pairs - 2):
        finish_keys(p)
    x_sum(last)
    for p in range(pairs - 2, pairs):
        finish_keys(p)
    wait_bytes(zr.at[pl.ds(0, NZ - 1)], bz_r)
    for p in range(pairs):
        total = zr[0, p].astype(F32)
        for d in range(1, NZ):
            total = total + zr[d, p].astype(F32)
        for r in range(16):
            dp_ref[15 - r : 16 - r, p * LANES : (p + 1) * LANES] = total[r : r + 1]

    wait_bytes(kvp, kv_s)
    wait_bytes(tab.at[:, 0, 0, 0], z_s)
    wait_bytes(tab.at[:, pl.ds(0, NY - 1), :, 0], y_s)
    wait_bytes(tab.at[:, :, :, 0], c_s)
    wait_bytes(dkv1, b_s)
    wait_bytes(corer, bc_s)
    wait_bytes(yr, by_s)
    wait_bytes(xr.at[pl.ds(0, NX - 1)], bx_s)
    wait_bytes(zr.at[pl.ds(0, NZ - 1)], bz_s)
    wait_bytes(dqv, out_sem.at[0])
    wait_bytes(dkvo, out_sem.at[1])


def write_out(*refs):
    sources, results, held, sems = refs[:4], refs[4:8], refs[8:12], refs[12]
    loads = [pltpu.make_async_copy(a, b, sems.at[0, n]) for n, (a, b) in enumerate(zip(sources, held))]
    stores = [pltpu.make_async_copy(a, b, sems.at[1, n]) for n, (a, b) in enumerate(zip(held, results))]
    for copy in loads:
        copy.start()
    for load, store in zip(loads, stores):
        load.wait()
        store.start()
    for copy in stores:
        copy.wait()


def local(query_rows, key_rows, value_rows, grad_out, pos_keys, bias_content, bias_position):
    width = query_rows.shape[2]
    pairs = width // LANES
    rows = query_rows.shape
    sem = pltpu.SemaphoreType.DMA
    hbm = pl.BlockSpec(memory_space=pltpu.HBM)
    vmem = pl.BlockSpec(memory_space=pltpu.VMEM)
    tile = (FRAMES, LANES)
    small = (16, LANES)
    gather, reduce = sem((len(GATHER),)), sem((len(REDUCE),))
    scratch = [
        pltpu.VMEM((pairs, *tile), BF16),
        pltpu.VMEM((pairs, 2, *tile), BF16),
        pltpu.VMEM((pairs, 4, *tile), BF16),
        pltpu.VMEM((16, width), BF16),
        pltpu.VMEM((2, 1, width), F32),
        pltpu.VMEM((pairs, 2, *tile), BF16),
        pltpu.VMEM((pairs, NY, 2, 2, *small), BF16),
        pltpu.VMEM((pairs, 2, *tile), F32),
        pltpu.VMEM((pairs, 2, *tile), BF16),
        pltpu.VMEM((pairs, 2, *tile), BF16),
        pltpu.VMEM((pairs, NY, 2, 2, *small), F32),
        pltpu.VMEM((pairs, NY, 2, 2, *small), BF16),
        pltpu.VMEM((pairs, NY, 2, *small), BF16),
        pltpu.VMEM((pairs, NY, 2, *small), BF16),
        pltpu.VMEM((NY - 1, pairs, 2, *small), BF16),
        pltpu.VMEM((NX, pairs, 2, *small), BF16),
        pltpu.VMEM((pairs, 2, *small), BF16),
        pltpu.VMEM((NZ, pairs, *small), BF16),
        sem((pairs,)),
        sem((3,)),
        sem, sem((pairs,)),
        sem, gather,
        sem, gather,
        sem, gather,
        sem, sem((pairs,)),
        sem, reduce,
        sem, reduce,
        sem, reduce,
        sem, sem,
        sem((2,)),
    ]
    wide = jax.ShapeDtypeStruct(rows, BF16)
    results = (wide, wide, wide, jax.ShapeDtypeStruct((16, width), F32))
    raw = pl.pallas_call(
        functools.partial(kernel, pairs),
        out_shape=results,
        in_specs=[hbm] * 7,
        out_specs=(hbm, hbm, hbm, vmem),
        scratch_shapes=scratch,
        compiler_params=pltpu.CompilerParams(
            collective_id=0, has_side_effects=True, vmem_limit_bytes=67_043_328
        ),
    )(
        query_rows, key_rows, value_rows, grad_out, pos_keys,
        bias_content.reshape(1, width), bias_position.reshape(1, width),
    )
    return pl.pallas_call(
        write_out,
        out_shape=results,
        in_specs=[hbm] * 4,
        out_specs=(hbm,) * 4,
        scratch_shapes=[pltpu.VMEM(a.shape, a.dtype) for a in results] + [sem((2, 4))],
        compiler_params=pltpu.CompilerParams(vmem_limit_bytes=67_043_328),
    )(*raw)


def solution(mesh):
    wide = P("dp", "blk", None)
    return jax.shard_map(
        local,
        mesh=mesh,
        in_specs=(wide, wide, wide, wide, P("blk", None), P(), P()),
        out_specs=(wide, wide, wide, P("blk", None)),
        check_vma=False,
    )
```

```python
import functools

import jax
import jax.numpy as jnp
from jax import lax
from jax.experimental import pallas as pl
from jax.experimental.pallas import tpu as pltpu
from jax.sharding import PartitionSpec as P

MESH = pl.DeviceIdType.MESH
DH = 64
LANES = 2 * DH
FRAMES = 128
F32, BF16 = jnp.float32, jnp.bfloat16
NX, NY, NZ, ZL = 4, 8, 8, 4
QUERY, GRAD, KEY, VALUE = range(4)
GATHER = ((0, 1), (1, 1), (2, 2), (4, 2), (6, 2))
SPLIT = 3
LAG = 1
TOGETHER = ((0,), (1,), (2,), (3,), (4, 5), (6,), (7,))
REDUCE = ((0, 2), (2, 1), (3, 1), (4, 1), (5, 1), (6, 1), (7, 1))


def contract_lanes(a, b):
    return lax.dot_general(a, b, (((1,), (1,)), ((), ())), preferred_element_type=F32)


def contract_rows(a, b):
    return lax.dot_general(a, b, (((0,), (0,)), ((), ())), preferred_element_type=F32)


def place_roll(d):
    rows = d.shape[0]
    shape = (FRAMES, FRAMES)
    flip = lax.broadcasted_iota(jnp.int32, shape, 0) + lax.broadcasted_iota(jnp.int32, shape, 1) == FRAMES - 1
    flip = jnp.where(flip, 1.0, 0.0).astype(BF16)

    def turned(m):
        return jnp.concatenate(
            [jnp.dot(flip, m[at : at + FRAMES], preferred_element_type=F32) for at in range(0, rows, FRAMES)], axis=0
        )

    upside = turned(d)
    rolled = [pltpu.roll(upside[:, at : at + FRAMES], 0, 1, stride=1, stride_axis=0) for at in (0, FRAMES)]
    placed = turned(jnp.concatenate(rolled, axis=1).astype(BF16)).astype(BF16)
    return placed[:, :FRAMES], placed[:, FRAMES:]


def pair_grads(q, grad, keys, values, table, bias_c, bias_p):
    first = lax.broadcasted_iota(jnp.int32, (FRAMES, LANES), 1) < DH

    def stacked(x):
        zero = jnp.zeros_like(x)
        both = jnp.concatenate([jnp.where(first, x, zero), jnp.where(first, zero, x)], axis=0)
        return both.astype(BF16)

    q32 = q.astype(F32)
    content_in = stacked(q32 + bias_c)
    position_in = stacked(q32 + bias_p)
    grad_in = stacked(grad.astype(F32))
    content = contract_lanes(content_in, keys)
    spread = contract_lanes(position_in, table)
    weights = contract_lanes(grad_in, values)
    shape = (2 * FRAMES, FRAMES)
    frame = lax.broadcasted_iota(jnp.int32, shape, 0) & (FRAMES - 1)
    upper = lax.broadcasted_iota(jnp.int32, shape, 1) + frame >= FRAMES - 1

    def select(at):
        picked = jnp.where(upper, spread[:, at : at + 128], spread[:, at + 128 : at + 256])
        return pltpu.roll(picked, 1, 1, stride=1, stride_axis=0)

    factor = DH**-0.5
    s0 = (content[:, :128] + select(256)) * factor
    s1 = (content[:, 128:] + select(0)) * factor
    top = jnp.max(jnp.maximum(s0, s1), axis=1, keepdims=True)
    e0, e1 = jnp.exp(s0 - top), jnp.exp(s1 - top)
    inverse = 1.0 / jnp.sum(e0 + e1, axis=1, keepdims=True)
    a0, a1 = e0 * inverse, e1 * inverse
    w0, w1 = weights[:, :128], weights[:, 128:]
    delta = jnp.sum(a0 * w0 + a1 * w1, axis=1, keepdims=True)
    d0 = a0 * (w0 - delta) * factor
    d1 = a1 * (w1 - delta) * factor
    dscore = jnp.concatenate([d0, d1], axis=1).astype(BF16)
    attention = jnp.concatenate([a0, a1], axis=1).astype(BF16)
    p0, p1 = place_roll(dscore)
    zero = jnp.zeros_like(p0)
    location = jnp.concatenate(
        [
            jnp.where(upper, p1, zero),
            jnp.where(upper, zero, p1),
            jnp.where(upper, p0, zero),
            jnp.where(upper, zero, p0),
        ],
        axis=1,
    )
    both = jnp.dot(
        jnp.concatenate([dscore, location], axis=1),
        jnp.concatenate([keys, table], axis=0),
        preferred_element_type=F32,
    )
    query_gradient = jnp.where(first, both[:FRAMES], both[FRAMES:])
    key_term = contract_rows(dscore, content_in)
    value_term = contract_rows(attention, grad_in)
    band_term = contract_rows(location, position_in)
    return query_gradient, key_term, value_term, band_term


def kernel(
    pairs,
    q_ref, k_ref, v_ref, g_ref, pos_ref, bc_ref, bp_ref,
    dq_ref, dk_ref, dv_ref, dp_ref,
    dqv, dkvo, inp, posv, biases, kvp, tab, dkv0, dkv1, dkv1r, band, band16, corer, ysend, yr, xr, zown, zr,
    in_sem, first_sem, kv_s, kv_r, z_s, z_r, y_s, y_r, h_s, h_r, c_s, c_r, b_s, b_r, bc_s, bc_r, by_s, by_r, bx_s, bx_r, bz_s, bz_r, out_sem,
):
    dp, blk = lax.axis_index("dp"), lax.axis_index("blk")
    x, zl = dp // ZL, dp % ZL
    y, zh, c = blk // 4, (blk // 2) % 2, blk % 2
    z = zh * ZL + zl
    count = 4 * NY

    def at(x_, y_, z_, c_):
        return (x_ * ZL + z_ % ZL, (y_ * 2 + z_ // ZL) * 2 + c_)

    following, before = (dp, (blk + 1) % count), (dp, (blk + count - 1) % count)
    partner = at(x, y, z, 1 - c)
    opposite = (dp, (y * 2 + 1 - zh) * 2 + c)
    y_peers = [at(x, (y + d) % NY, z, c) for d in range(1, NY)]
    x_peers = [at((x + d) % NX, y, z, c) for d in range(1, NX)]
    z_peers = [at(x, y, (z + d) % NZ, c) for d in range(1, NZ)]
    y_order = (3, 2, 4, 1, 5, 0, 6)

    def remote(src, dst, send, recv, device):
        return pltpu.make_async_remote_copy(
            src_ref=src, dst_ref=dst, send_sem=send, recv_sem=recv, device_id=device, device_id_type=MESH
        )

    def wait_bytes(ref, sem):
        pltpu.make_async_copy(ref, ref, sem).wait()

    def cols(p):
        return pl.ds(p * LANES, LANES)

    def chunk(k, chunks):
        return pl.ds(*chunks[k])

    barrier = pltpu.get_barrier_semaphore()
    peers = [following, before] + y_peers + x_peers + z_peers
    for peer in peers:
        pl.semaphore_signal(barrier, inc=1, device_id=peer, device_id_type=MESH)
    pos_copy = pltpu.make_async_copy(pos_ref, posv, first_sem.at[0])
    pos_copy.start()
    bias_copies = [
        pltpu.make_async_copy(ref, biases.at[n], first_sem.at[1 + n]) for n, ref in enumerate((bc_ref, bp_ref))
    ]
    for copy in bias_copies:
        copy.start()

    flip = (
        lax.broadcasted_iota(jnp.int32, (16, 16), 0) + lax.broadcasted_iota(jnp.int32, (16, 16), 1) == 15
    )
    pos_copy.wait()
    turned = jnp.dot(
        jnp.where(flip, 1.0, 0.0).astype(BF16), posv[...], preferred_element_type=F32
    ).astype(BF16)
    sy, sz, sc = NY - 1 - y, 1 - zh, 1 - c
    split_from = GATHER[SPLIT][0]
    for p in range(pairs):
        rows = turned[:, p * LANES : (p + 1) * LANES]
        if p < split_from:
            tab[p, sy, sz, sc] = rows
        else:

            @pl.when(x == p - split_from)
            def _(p=p, rows=rows):
                tab[p, sy, sz, sc] = rows
    for copy in bias_copies:
        copy.wait()
    pl.semaphore_wait(barrier, len(peers))

    own_pair = pl.ds(GATHER[SPLIT][0] + x, 1)

    def gathered(k):
        return own_pair if k == SPLIT else chunk(k, GATHER)

    def shard(k, z_):
        return tab.at[gathered(k), sy, z_, sc]

    def along_y(k, z_):
        for d in y_order:
            remote(shard(k, z_), shard(k, z_), y_s, y_r.at[k], y_peers[d]).start()

    def shift(k):
        for p in range(GATHER[k][0], sum(GATHER[k])):
            for n, ref in ((0, k_ref), (1, v_ref)):
                remote(ref.at[0, :, cols(p)], kvp.at[p, n], kv_s, kv_r.at[p], following).start()

    chunks = len(GATHER)

    def pass_on(k):
        wait_bytes(shard(k, 1 - sz), z_r.at[k])
        along_y(k, 1 - sz)

    for k in range(SPLIT + 1):
        remote(shard(k, sz), shard(k, sz), z_s, z_r.at[k], opposite).start()
    for k in (0, 1):
        along_y(k, sz)
        shift(k)
    along_y(SPLIT, sz)
    along_y(2, sz)
    for p in range(pairs):
        for n, ref in ((QUERY, q_ref), (GRAD, g_ref), (KEY, k_ref), (VALUE, v_ref)):
            pltpu.make_async_copy(ref.at[0, :, cols(p)], inp.at[p, n], in_sem.at[p]).start()
    for k in (0, 1, SPLIT, 2):
        pass_on(k)
    for k in range(2, chunks):
        shift(k)

    def gather_wait(k):
        wait_bytes(tab.at[gathered(k), pl.ds(0, NY - 1), :, 0], y_r.at[k])

    def hand_round():
        gather_wait(SPLIT)
        rows = tab.at[own_pair, :, :, sc]
        for peer in x_peers:
            remote(rows, rows, h_s, h_r, peer).start()

    def share_table(k):
        mine = tab.at[chunk(k, GATHER), :, :, sc]
        remote(mine, mine, c_s, c_r.at[k], partner).start()

    def pair_steps(*ps):
        for p in ps:
            wait_bytes(inp.at[p], in_sem.at[p])
            wait_bytes(kvp.at[p], kv_r.at[p])
        for p in ps:
            keys = jnp.concatenate([inp[p, KEY], kvp[p, 0]], axis=0)
            values = jnp.concatenate([inp[p, VALUE], kvp[p, 1]], axis=0)
            table = tab[p].reshape(32 * 16, LANES)
            lanes = slice(p * LANES, (p + 1) * LANES)
            dq, dk, dv, db = pair_grads(
                inp[p, QUERY], inp[p, GRAD], keys, values, table, biases[0, :, lanes], biases[1, :, lanes]
            )
            dqv[p] = dq.astype(BF16)
            dkv0[p, 0] = dk[:FRAMES]
            dkv0[p, 1] = dv[:FRAMES]
            dkv1[p, 0] = dk[FRAMES:].astype(BF16)
            dkv1[p, 1] = dv[FRAMES:].astype(BF16)
            db = db.reshape(NY, 2, 2, 16, LANES)
            band[p] = db
            band16[p] = db.astype(BF16)
        for p in ps:
            pltpu.make_async_copy(dqv.at[p], dq_ref.at[0, :, cols(p)], out_sem.at[0]).start()

    def send_back(k):
        part = chunk(k, REDUCE)
        remote(band16.at[part, :, :, c], corer.at[part], bc_s, bc_r.at[k], partner).start()
        for p in range(REDUCE[k][0], sum(REDUCE[k])):
            remote(dkv1.at[p], dkv1r.at[p], b_s, b_r.at[p], before).start()

    def chip_sum(k):
        part = chunk(k, REDUCE)
        wait_bytes(corer.at[part], bc_r.at[k])
        for p in range(REDUCE[k][0], sum(REDUCE[k])):
            total = band[p, :, :, sc] + corer[p].astype(F32)
            ysend[p] = total.astype(BF16)
        for d in y_order:
            sink = NY - 1 - (y + d + 1) % NY
            remote(ysend.at[part, sink], yr.at[d, part], by_s, by_r.at[k], y_peers[d]).start()

    def y_sum(k):
        part = chunk(k, REDUCE)
        wait_bytes(yr.at[:, part], by_r.at[k])
        for p in range(REDUCE[k][0], sum(REDUCE[k])):
            total = band[p, sy, :, sc] + corer[p, sy].astype(F32)
            for d in range(NY - 1):
                total = total + yr[d, p].astype(F32)
            xr[x, p] = total.astype(BF16)
        for peer in x_peers:
            remote(xr.at[x, part], xr.at[x, part], bx_s, bx_r.at[k], peer).start()

    def x_sum(k):
        part = chunk(k, REDUCE)
        wait_bytes(xr.at[pl.ds(0, NX - 1), part], bx_r.at[k])
        for p in range(REDUCE[k][0], sum(REDUCE[k])):
            total = xr[0, p].astype(F32)
            for d in range(1, NX):
                total = total + xr[d, p].astype(F32)
            zown[p] = total.astype(BF16)
            zr[z, p] = zown[p, sz]
        for d, peer in enumerate(z_peers):
            half = (z + d + 1) % NZ // ZL
            remote(zown.at[part, 1 - half], zr.at[z, part], bz_s, bz_r, peer).start()

    def finish_keys(p):
        wait_bytes(dkv1r.at[p], b_r.at[p])
        dkvo[p] = (dkv0[p] + dkv1r[p].astype(F32)).astype(BF16)
        for n, ref in ((0, dk_ref), (1, dv_ref)):
            pltpu.make_async_copy(dkvo.at[p, n], ref.at[0, :, cols(p)], out_sem.at[1]).start()

    done = summed = 0
    for k in (0, 1):
        gather_wait(k)
        share_table(k)
    hand_round()

    def table_wait(k):
        wait_bytes(tab.at[chunk(k, GATHER), :, :, 0], c_r.at[k])

    for ps in TOGETHER:
        for k, (start, _) in enumerate(GATHER):
            if start in ps:
                table_wait(k)
        pair_steps(*ps)
        if 0 in ps:
            gather_wait(2)
            share_table(2)
        if 2 in ps:
            wait_bytes(tab.at[pl.ds(0, NX - 1), :, :, 0], h_r)
            for later in range(SPLIT, chunks):
                share_table(later)
        while done < len(REDUCE) and sum(REDUCE[done]) - 1 <= ps[-1]:
            send_back(done)
            done += 1
        while summed < done - LAG:
            chip_sum(summed)
            summed += 1
    last = len(REDUCE) - 1
    y_sum(0)
    for k in range(summed, last + 1):
        chip_sum(k)
    for k in range(1, last + 1):
        y_sum(k)
        if k >= 2:
            x_sum(k - 2)
    x_sum(last - 1)
    for p in range(pairs - 2):
        finish_keys(p)
    x_sum(last)
    for p in range(pairs - 2, pairs):
        finish_keys(p)
    wait_bytes(zr.at[pl.ds(0, NZ - 1)], bz_r)
    for p in range(pairs):
        total = zr[0, p].astype(F32)
        for d in range(1, NZ):
            total = total + zr[d, p].astype(F32)
        for r in range(16):
            dp_ref[15 - r : 16 - r, p * LANES : (p + 1) * LANES] = total[r : r + 1]

    wait_bytes(kvp, kv_s)
    sent = pl.ds(0, GATHER[SPLIT][0] + 1)
    wait_bytes(tab.at[sent, 0, 0, 0], z_s)
    wait_bytes(tab.at[sent, pl.ds(0, NY - 1), :, 0], y_s)
    wait_bytes(tab.at[pl.ds(0, NX - 1), :, :, 0], h_s)
    wait_bytes(tab.at[:, :, :, 0], c_s)
    wait_bytes(dkv1, b_s)
    wait_bytes(corer, bc_s)
    wait_bytes(yr, by_s)
    wait_bytes(xr.at[pl.ds(0, NX - 1)], bx_s)
    wait_bytes(zr.at[pl.ds(0, NZ - 1)], bz_s)
    wait_bytes(dqv, out_sem.at[0])
    wait_bytes(dkvo, out_sem.at[1])


def write_out(*refs):
    sources, results, held, sems = refs[:4], refs[4:8], refs[8:12], refs[12]
    loads = [pltpu.make_async_copy(a, b, sems.at[0, n]) for n, (a, b) in enumerate(zip(sources, held))]
    stores = [pltpu.make_async_copy(a, b, sems.at[1, n]) for n, (a, b) in enumerate(zip(held, results))]
    for copy in loads:
        copy.start()
    for load, store in zip(loads, stores):
        load.wait()
        store.start()
    for copy in stores:
        copy.wait()


def local(query_rows, key_rows, value_rows, grad_out, pos_keys, bias_content, bias_position):
    width = query_rows.shape[2]
    pairs = width // LANES
    rows = query_rows.shape
    sem = pltpu.SemaphoreType.DMA
    hbm = pl.BlockSpec(memory_space=pltpu.HBM)
    vmem = pl.BlockSpec(memory_space=pltpu.VMEM)
    tile = (FRAMES, LANES)
    small = (16, LANES)
    gather, reduce = sem((len(GATHER),)), sem((len(REDUCE),))
    scratch = [
        pltpu.VMEM((pairs, *tile), BF16),
        pltpu.VMEM((pairs, 2, *tile), BF16),
        pltpu.VMEM((pairs, 4, *tile), BF16),
        pltpu.VMEM((16, width), BF16),
        pltpu.VMEM((2, 1, width), F32),
        pltpu.VMEM((pairs, 2, *tile), BF16),
        pltpu.VMEM((pairs, NY, 2, 2, *small), BF16),
        pltpu.VMEM((pairs, 2, *tile), F32),
        pltpu.VMEM((pairs, 2, *tile), BF16),
        pltpu.VMEM((pairs, 2, *tile), BF16),
        pltpu.VMEM((pairs, NY, 2, 2, *small), F32),
        pltpu.VMEM((pairs, NY, 2, 2, *small), BF16),
        pltpu.VMEM((pairs, NY, 2, *small), BF16),
        pltpu.VMEM((pairs, NY, 2, *small), BF16),
        pltpu.VMEM((NY - 1, pairs, 2, *small), BF16),
        pltpu.VMEM((NX, pairs, 2, *small), BF16),
        pltpu.VMEM((pairs, 2, *small), BF16),
        pltpu.VMEM((NZ, pairs, *small), BF16),
        sem((pairs,)),
        sem((3,)),
        sem, sem((pairs,)),
        sem, gather,
        sem, gather,
        sem, sem,
        sem, gather,
        sem, sem((pairs,)),
        sem, reduce,
        sem, reduce,
        sem, reduce,
        sem, sem,
        sem((2,)),
    ]
    wide = jax.ShapeDtypeStruct(rows, BF16)
    results = (wide, wide, wide, jax.ShapeDtypeStruct((16, width), F32))
    raw = pl.pallas_call(
        functools.partial(kernel, pairs),
        out_shape=results,
        in_specs=[hbm] * 7,
        out_specs=(hbm, hbm, hbm, vmem),
        scratch_shapes=scratch,
        compiler_params=pltpu.CompilerParams(
            collective_id=0, has_side_effects=True, vmem_limit_bytes=67_043_328
        ),
    )(
        query_rows, key_rows, value_rows, grad_out, pos_keys,
        bias_content.reshape(1, width), bias_position.reshape(1, width),
    )
    return pl.pallas_call(
        write_out,
        out_shape=results,
        in_specs=[hbm] * 4,
        out_specs=(hbm,) * 4,
        scratch_shapes=[pltpu.VMEM(a.shape, a.dtype) for a in results] + [sem((2, 4))],
        compiler_params=pltpu.CompilerParams(vmem_limit_bytes=67_043_328),
    )(*raw)


def solution(mesh):
    wide = P("dp", "blk", None)
    return jax.shard_map(
        local,
        mesh=mesh,
        in_specs=(wide, wide, wide, wide, P("blk", None), P(), P()),
        out_specs=(wide, wide, wide, P("blk", None)),
        check_vma=False,
    )
```

```python
import functools

import jax
import jax.numpy as jnp
from jax import lax
from jax.experimental import pallas as pl
from jax.experimental.pallas import tpu as pltpu
from jax.sharding import PartitionSpec as P

MESH = pl.DeviceIdType.MESH
DH = 64
LANES = 2 * DH
FRAMES = 128
F32, BF16 = jnp.float32, jnp.bfloat16
NX, NY, NZ, ZL = 4, 8, 8, 4
QUERY, GRAD, KEY, VALUE = range(4)
GATHER = ((0, 1), (1, 1), (2, 2), (4, 2), (6, 2))
SPLIT = 3
LAG = 1
TOGETHER = ((0,), (1,), (2,), (3,), (4, 5), (6,), (7,))
REDUCE = ((0, 1), (1, 1), (2, 1), (3, 1), (4, 1), (5, 1), (6, 1), (7, 1))


def contract_lanes(a, b):
    return lax.dot_general(a, b, (((1,), (1,)), ((), ())), preferred_element_type=F32)


def contract_rows(a, b):
    return lax.dot_general(a, b, (((0,), (0,)), ((), ())), preferred_element_type=F32)


def place_roll(d):
    rows = d.shape[0]
    shape = (FRAMES, FRAMES)
    flip = lax.broadcasted_iota(jnp.int32, shape, 0) + lax.broadcasted_iota(jnp.int32, shape, 1) == FRAMES - 1
    flip = jnp.where(flip, 1.0, 0.0).astype(BF16)

    def turned(m):
        return jnp.concatenate(
            [jnp.dot(flip, m[at : at + FRAMES], preferred_element_type=F32) for at in range(0, rows, FRAMES)], axis=0
        )

    upside = turned(d)
    rolled = [pltpu.roll(upside[:, at : at + FRAMES], 0, 1, stride=1, stride_axis=0) for at in (0, FRAMES)]
    placed = turned(jnp.concatenate(rolled, axis=1).astype(BF16)).astype(BF16)
    return placed[:, :FRAMES], placed[:, FRAMES:]


def pair_grads(q, grad, keys, values, table, bias_c, bias_p):
    first = lax.broadcasted_iota(jnp.int32, (FRAMES, LANES), 1) < DH

    def stacked(x):
        zero = jnp.zeros_like(x)
        both = jnp.concatenate([jnp.where(first, x, zero), jnp.where(first, zero, x)], axis=0)
        return both.astype(BF16)

    q32 = q.astype(F32)
    content_in = stacked(q32 + bias_c)
    position_in = stacked(q32 + bias_p)
    grad_in = stacked(grad.astype(F32))
    content = contract_lanes(content_in, keys)
    spread = contract_lanes(position_in, table)
    weights = contract_lanes(grad_in, values)
    shape = (2 * FRAMES, FRAMES)
    frame = lax.broadcasted_iota(jnp.int32, shape, 0) & (FRAMES - 1)
    upper = lax.broadcasted_iota(jnp.int32, shape, 1) + frame >= FRAMES - 1

    def select(at):
        picked = jnp.where(upper, spread[:, at : at + 128], spread[:, at + 128 : at + 256])
        return pltpu.roll(picked, 1, 1, stride=1, stride_axis=0)

    factor = DH**-0.5
    s0 = (content[:, :128] + select(256)) * factor
    s1 = (content[:, 128:] + select(0)) * factor
    top = jnp.max(jnp.maximum(s0, s1), axis=1, keepdims=True)
    e0, e1 = jnp.exp(s0 - top), jnp.exp(s1 - top)
    inverse = 1.0 / jnp.sum(e0 + e1, axis=1, keepdims=True)
    a0, a1 = e0 * inverse, e1 * inverse
    w0, w1 = weights[:, :128], weights[:, 128:]
    delta = jnp.sum(a0 * w0 + a1 * w1, axis=1, keepdims=True)
    d0 = a0 * (w0 - delta) * factor
    d1 = a1 * (w1 - delta) * factor
    dscore = jnp.concatenate([d0, d1], axis=1).astype(BF16)
    attention = jnp.concatenate([a0, a1], axis=1).astype(BF16)
    p0, p1 = place_roll(dscore)
    zero = jnp.zeros_like(p0)
    location = jnp.concatenate(
        [
            jnp.where(upper, p1, zero),
            jnp.where(upper, zero, p1),
            jnp.where(upper, p0, zero),
            jnp.where(upper, zero, p0),
        ],
        axis=1,
    )
    both = jnp.dot(
        jnp.concatenate([dscore, location], axis=1),
        jnp.concatenate([keys, table], axis=0),
        preferred_element_type=F32,
    )
    query_gradient = jnp.where(first, both[:FRAMES], both[FRAMES:])
    key_term = contract_rows(dscore, content_in)
    value_term = contract_rows(attention, grad_in)
    band_term = contract_rows(location, position_in)
    return query_gradient, key_term, value_term, band_term


def kernel(
    pairs,
    q_ref, k_ref, v_ref, g_ref, pos_ref, bc_ref, bp_ref,
    dq_ref, dk_ref, dv_ref, dp_ref,
    dqv, dkvo, inp, posv, biases, kvp, tab, dkv0, dkv1, dkv1r, band, band16, corer, ysend, yr, xr, zown, zr,
    in_sem, first_sem, kv_s, kv_r, z_s, z_r, y_s, y_r, h_s, h_r, c_s, c_r, b_s, b_r, bc_s, bc_r, by_s, by_r, bx_s, bx_r, bz_s, bz_r, out_sem,
):
    dp, blk = lax.axis_index("dp"), lax.axis_index("blk")
    x, zl = dp // ZL, dp % ZL
    y, zh, c = blk // 4, (blk // 2) % 2, blk % 2
    z = zh * ZL + zl
    count = 4 * NY

    def at(x_, y_, z_, c_):
        return (x_ * ZL + z_ % ZL, (y_ * 2 + z_ // ZL) * 2 + c_)

    following, before = (dp, (blk + 1) % count), (dp, (blk + count - 1) % count)
    partner = at(x, y, z, 1 - c)
    opposite = (dp, (y * 2 + 1 - zh) * 2 + c)
    y_peers = [at(x, (y + d) % NY, z, c) for d in range(1, NY)]
    x_peers = [at((x + d) % NX, y, z, c) for d in range(1, NX)]
    z_peers = [at(x, y, (z + d) % NZ, c) for d in range(1, NZ)]
    y_order = (3, 2, 4, 1, 5, 0, 6)

    def remote(src, dst, send, recv, device):
        return pltpu.make_async_remote_copy(
            src_ref=src, dst_ref=dst, send_sem=send, recv_sem=recv, device_id=device, device_id_type=MESH
        )

    def wait_bytes(ref, sem):
        pltpu.make_async_copy(ref, ref, sem).wait()

    def cols(p):
        return pl.ds(p * LANES, LANES)

    def chunk(k, chunks):
        return pl.ds(*chunks[k])

    pos_copy = pltpu.make_async_copy(pos_ref, posv, first_sem.at[0])
    pos_copy.start()
    barrier = pltpu.get_barrier_semaphore()
    peers = [following, before] + y_peers + x_peers + z_peers
    for peer in peers:
        pl.semaphore_signal(barrier, inc=1, device_id=peer, device_id_type=MESH)
    bias_copies = [
        pltpu.make_async_copy(ref, biases.at[n], first_sem.at[1 + n]) for n, ref in enumerate((bc_ref, bp_ref))
    ]
    for copy in bias_copies:
        copy.start()

    flip = (
        lax.broadcasted_iota(jnp.int32, (16, 16), 0) + lax.broadcasted_iota(jnp.int32, (16, 16), 1) == 15
    )
    pos_copy.wait()
    turned = jnp.dot(
        jnp.where(flip, 1.0, 0.0).astype(BF16), posv[...], preferred_element_type=F32
    ).astype(BF16)
    sy, sz, sc = NY - 1 - y, 1 - zh, 1 - c
    split_from = GATHER[SPLIT][0]
    for p in range(pairs):
        rows = turned[:, p * LANES : (p + 1) * LANES]
        if p < split_from:
            tab[p, sy, sz, sc] = rows
        else:

            @pl.when(x == p - split_from)
            def _(p=p, rows=rows):
                tab[p, sy, sz, sc] = rows
    for copy in bias_copies:
        copy.wait()
    pl.semaphore_wait(barrier, len(peers))

    own_pair = pl.ds(GATHER[SPLIT][0] + x, 1)

    def gathered(k):
        return own_pair if k == SPLIT else chunk(k, GATHER)

    def shard(k, z_):
        return tab.at[gathered(k), sy, z_, sc]

    def along_y(k, z_):
        for d in y_order:
            remote(shard(k, z_), shard(k, z_), y_s, y_r.at[k], y_peers[d]).start()

    def shift(k):
        for p in range(GATHER[k][0], sum(GATHER[k])):
            for n, ref in ((0, k_ref), (1, v_ref)):
                remote(ref.at[0, :, cols(p)], kvp.at[p, n], kv_s, kv_r.at[p], following).start()

    chunks = len(GATHER)

    def pass_on(k):
        wait_bytes(shard(k, 1 - sz), z_r.at[k])
        along_y(k, 1 - sz)

    for k in range(SPLIT + 1):
        remote(shard(k, sz), shard(k, sz), z_s, z_r.at[k], opposite).start()
    for k in (0, 1):
        along_y(k, sz)
        shift(k)
    along_y(SPLIT, sz)
    along_y(2, sz)
    for p in range(pairs):
        for n, ref in ((QUERY, q_ref), (GRAD, g_ref), (KEY, k_ref), (VALUE, v_ref)):
            pltpu.make_async_copy(ref.at[0, :, cols(p)], inp.at[p, n], in_sem.at[p]).start()
    for k in (0, 1, SPLIT, 2):
        pass_on(k)
    for k in range(2, chunks):
        shift(k)

    def gather_wait(k):
        wait_bytes(tab.at[gathered(k), pl.ds(0, NY - 1), :, 0], y_r.at[k])

    def hand_round():
        gather_wait(SPLIT)
        rows = tab.at[own_pair, :, :, sc]
        for peer in x_peers:
            remote(rows, rows, h_s, h_r, peer).start()

    def share_table(k):
        mine = tab.at[chunk(k, GATHER), :, :, sc]
        remote(mine, mine, c_s, c_r.at[k], partner).start()

    def pair_steps(*ps):
        for p in ps:
            wait_bytes(inp.at[p], in_sem.at[p])
            wait_bytes(kvp.at[p], kv_r.at[p])
        for p in ps:
            keys = jnp.concatenate([inp[p, KEY], kvp[p, 0]], axis=0)
            values = jnp.concatenate([inp[p, VALUE], kvp[p, 1]], axis=0)
            table = tab[p].reshape(32 * 16, LANES)
            lanes = slice(p * LANES, (p + 1) * LANES)
            dq, dk, dv, db = pair_grads(
                inp[p, QUERY], inp[p, GRAD], keys, values, table, biases[0, :, lanes], biases[1, :, lanes]
            )
            dqv[p] = dq.astype(BF16)
            dkv0[p, 0] = dk[:FRAMES]
            dkv0[p, 1] = dv[:FRAMES]
            dkv1[p, 0] = dk[FRAMES:].astype(BF16)
            dkv1[p, 1] = dv[FRAMES:].astype(BF16)
            db = db.reshape(NY, 2, 2, 16, LANES)
            band[p] = db
            band16[p] = db.astype(BF16)
        for p in ps:
            pltpu.make_async_copy(dqv.at[p], dq_ref.at[0, :, cols(p)], out_sem.at[0]).start()

    def send_back(k):
        part = chunk(k, REDUCE)
        remote(band16.at[part, :, :, c], corer.at[part], bc_s, bc_r.at[k], partner).start()
        for p in range(REDUCE[k][0], sum(REDUCE[k])):
            remote(dkv1.at[p], dkv1r.at[p], b_s, b_r.at[p], before).start()

    def chip_sum(k):
        part = chunk(k, REDUCE)
        wait_bytes(corer.at[part], bc_r.at[k])
        for p in range(REDUCE[k][0], sum(REDUCE[k])):
            total = band[p, :, :, sc] + corer[p].astype(F32)
            ysend[p] = total.astype(BF16)
        for d in y_order:
            sink = NY - 1 - (y + d + 1) % NY
            remote(ysend.at[part, sink], yr.at[d, part], by_s, by_r.at[k], y_peers[d]).start()

    def y_sum(k):
        part = chunk(k, REDUCE)
        wait_bytes(yr.at[:, part], by_r.at[k])
        for p in range(REDUCE[k][0], sum(REDUCE[k])):
            total = band[p, sy, :, sc] + corer[p, sy].astype(F32)
            for d in range(NY - 1):
                total = total + yr[d, p].astype(F32)
            xr[x, p] = total.astype(BF16)
        for peer in x_peers:
            remote(xr.at[x, part], xr.at[x, part], bx_s, bx_r.at[k], peer).start()

    def x_sum(k):
        part = chunk(k, REDUCE)
        wait_bytes(xr.at[pl.ds(0, NX - 1), part], bx_r.at[k])
        for p in range(REDUCE[k][0], sum(REDUCE[k])):
            total = xr[0, p].astype(F32)
            for d in range(1, NX):
                total = total + xr[d, p].astype(F32)
            zown[p] = total.astype(BF16)
            zr[z, p] = zown[p, sz]
        for d, peer in enumerate(z_peers):
            half = (z + d + 1) % NZ // ZL
            remote(zown.at[part, 1 - half], zr.at[z, part], bz_s, bz_r, peer).start()

    def finish_keys(p):
        wait_bytes(dkv1r.at[p], b_r.at[p])
        dkvo[p] = (dkv0[p] + dkv1r[p].astype(F32)).astype(BF16)
        for n, ref in ((0, dk_ref), (1, dv_ref)):
            pltpu.make_async_copy(dkvo.at[p, n], ref.at[0, :, cols(p)], out_sem.at[1]).start()

    done = summed = 0
    for k in (0, 1):
        gather_wait(k)
        share_table(k)
    hand_round()

    def table_wait(k):
        wait_bytes(tab.at[chunk(k, GATHER), :, :, 0], c_r.at[k])

    for ps in TOGETHER:
        for k, (start, _) in enumerate(GATHER):
            if start in ps:
                table_wait(k)
        pair_steps(*ps)
        if 0 in ps:
            gather_wait(2)
            share_table(2)
        if 2 in ps:
            wait_bytes(tab.at[pl.ds(0, NX - 1), :, :, 0], h_r)
            for later in range(SPLIT, chunks):
                share_table(later)
        while done < len(REDUCE) and sum(REDUCE[done]) - 1 <= ps[-1]:
            send_back(done)
            done += 1
        while summed < done - LAG:
            chip_sum(summed)
            summed += 1
    last = len(REDUCE) - 1
    y_sum(0)
    for k in range(summed, last + 1):
        chip_sum(k)
    for k in range(1, last + 1):
        y_sum(k)
        if k >= 2:
            x_sum(k - 2)
    x_sum(last - 1)
    for p in range(pairs - 2):
        finish_keys(p)
    x_sum(last)
    for p in range(pairs - 2, pairs):
        finish_keys(p)
    wait_bytes(zr.at[pl.ds(0, NZ - 1)], bz_r)
    for p in range(pairs):
        total = zr[0, p].astype(F32)
        for d in range(1, NZ):
            total = total + zr[d, p].astype(F32)
        for r in range(16):
            dp_ref[15 - r : 16 - r, p * LANES : (p + 1) * LANES] = total[r : r + 1]

    wait_bytes(kvp, kv_s)
    sent = pl.ds(0, GATHER[SPLIT][0] + 1)
    wait_bytes(tab.at[sent, 0, 0, 0], z_s)
    wait_bytes(tab.at[sent, pl.ds(0, NY - 1), :, 0], y_s)
    wait_bytes(tab.at[pl.ds(0, NX - 1), :, :, 0], h_s)
    wait_bytes(tab.at[:, :, :, 0], c_s)
    wait_bytes(dkv1, b_s)
    wait_bytes(corer, bc_s)
    wait_bytes(yr, by_s)
    wait_bytes(xr.at[pl.ds(0, NX - 1)], bx_s)
    wait_bytes(zr.at[pl.ds(0, NZ - 1)], bz_s)
    wait_bytes(dqv, out_sem.at[0])
    wait_bytes(dkvo, out_sem.at[1])


def write_out(*refs):
    sources, results, held, sems = refs[:4], refs[4:8], refs[8:12], refs[12]
    loads = [pltpu.make_async_copy(a, b, sems.at[0, n]) for n, (a, b) in enumerate(zip(sources, held))]
    stores = [pltpu.make_async_copy(a, b, sems.at[1, n]) for n, (a, b) in enumerate(zip(held, results))]
    for copy in loads:
        copy.start()
    for load, store in zip(loads, stores):
        load.wait()
        store.start()
    for copy in stores:
        copy.wait()


def local(query_rows, key_rows, value_rows, grad_out, pos_keys, bias_content, bias_position):
    width = query_rows.shape[2]
    pairs = width // LANES
    rows = query_rows.shape
    sem = pltpu.SemaphoreType.DMA
    hbm = pl.BlockSpec(memory_space=pltpu.HBM)
    vmem = pl.BlockSpec(memory_space=pltpu.VMEM)
    tile = (FRAMES, LANES)
    small = (16, LANES)
    gather, reduce = sem((len(GATHER),)), sem((len(REDUCE),))
    scratch = [
        pltpu.VMEM((pairs, *tile), BF16),
        pltpu.VMEM((pairs, 2, *tile), BF16),
        pltpu.VMEM((pairs, 4, *tile), BF16),
        pltpu.VMEM((16, width), BF16),
        pltpu.VMEM((2, 1, width), F32),
        pltpu.VMEM((pairs, 2, *tile), BF16),
        pltpu.VMEM((pairs, NY, 2, 2, *small), BF16),
        pltpu.VMEM((pairs, 2, *tile), F32),
        pltpu.VMEM((pairs, 2, *tile), BF16),
        pltpu.VMEM((pairs, 2, *tile), BF16),
        pltpu.VMEM((pairs, NY, 2, 2, *small), F32),
        pltpu.VMEM((pairs, NY, 2, 2, *small), BF16),
        pltpu.VMEM((pairs, NY, 2, *small), BF16),
        pltpu.VMEM((pairs, NY, 2, *small), BF16),
        pltpu.VMEM((NY - 1, pairs, 2, *small), BF16),
        pltpu.VMEM((NX, pairs, 2, *small), BF16),
        pltpu.VMEM((pairs, 2, *small), BF16),
        pltpu.VMEM((NZ, pairs, *small), BF16),
        sem((pairs,)),
        sem((3,)),
        sem, sem((pairs,)),
        sem, gather,
        sem, gather,
        sem, sem,
        sem, gather,
        sem, sem((pairs,)),
        sem, reduce,
        sem, reduce,
        sem, reduce,
        sem, sem,
        sem((2,)),
    ]
    wide = jax.ShapeDtypeStruct(rows, BF16)
    results = (wide, wide, wide, jax.ShapeDtypeStruct((16, width), F32))
    raw = pl.pallas_call(
        functools.partial(kernel, pairs),
        out_shape=results,
        in_specs=[hbm] * 7,
        out_specs=(hbm, hbm, hbm, vmem),
        scratch_shapes=scratch,
        compiler_params=pltpu.CompilerParams(
            collective_id=0, has_side_effects=True, vmem_limit_bytes=67_043_328
        ),
    )(
        query_rows, key_rows, value_rows, grad_out, pos_keys,
        bias_content.reshape(1, width), bias_position.reshape(1, width),
    )
    return pl.pallas_call(
        write_out,
        out_shape=results,
        in_specs=[hbm] * 4,
        out_specs=(hbm,) * 4,
        scratch_shapes=[pltpu.VMEM(a.shape, a.dtype) for a in results] + [sem((2, 4))],
        compiler_params=pltpu.CompilerParams(vmem_limit_bytes=67_043_328),
    )(*raw)


def solution(mesh):
    wide = P("dp", "blk", None)
    return jax.shard_map(
        local,
        mesh=mesh,
        in_specs=(wide, wide, wide, wide, P("blk", None), P(), P()),
        out_specs=(wide, wide, wide, P("blk", None)),
        check_vma=False,
    )
```
